256 devices in a mesh: tm: 32 (over z, x), rows: 8 (over y, core).
Axes of the slice: x: 4, y: 4, z: 8, core: 2. Of those that a mesh axis runs over, the one named last changes fastest.
Arguments:
- observations: float32 [32, 2048], P('tm'), may hold values from -48 to 48
- site_ids: int32 [32, 2048], P('tm'), may hold values from 0 to 4095
- counts: int32 [32], P('tm'), may hold values from 1 to 2048, 49152 in all
- frequencies: float32 [128], replicated, may hold values from -3.140625 to 3.140625
- decay: float32 [128], replicated, may hold values from 0.02 to 0.2
- proc_var: float32 [128], replicated, may hold values from 0.05 to 0.2
Outputs:
- smooth_mean: float32 [32, 256], P('tm', 'rows')
- smooth_cov: float32 [32, 256, 256], P('tm', 'rows')
The draws below stay inside these ranges and needn't reach their ends.
Inputs may be any that keep to these rules, and one draw needn't show every extreme that they name: Step t observes the sites in its first counts[t] slots; the other slots are ignored.
All inputs are finite; a program needn't handle non-finite values. No bound on the sum of `counts` on one device may be relied on, other than what follows from the above.
Results may differ from the reference program's by a relative error of at most 0.0003.
Values sent between devices are 32-bit elements; how exact they have to be, the bound alone decides.
No kernel may reach another device: no remote copies, remote signals or barrier semaphores. Data moves between devices by JAX's collectives and lax.ppermute only.
A program may use at most 128 MiB of HBM per device.

```python
import math
import jax
import jax.numpy as jnp
import numpy as np
from jax import lax

MODES = 128
SITES = 2048
GRID = 4096
OBS_VAR = 64
STEPS = 32


def with_ends(result, stream_key, low, top_value):
    longest = result.shape.index(max(result.shape))
    spots = []
    for shift in (0, 1):
        where = [jax.random.randint(jax.random.fold_in(stream_key, axis), (), 0, length) for axis, length in enumerate(result.shape)]
        where[longest] = (where[longest] + shift) % result.shape[longest]
        spots.append(tuple(where))
    return result.at[spots[0]].set(low).at[spots[1]].set(top_value)


def steps_of(rng, dims, shards, smallest, high):
    def one(axis_at, blocks):
        heights = jax.random.uniform(jax.random.fold_in(jax.random.fold_in(rng, 6), axis_at), (blocks,), jnp.float32, smallest / len(shards), high / len(shards))
        return jnp.repeat(jnp.exp(heights), dims[axis_at] // blocks).reshape((-1,) + (1,) * (len(dims) - axis_at - 1))

    loudness = one(*shards[0])
    for cut in shards[1:]:
        loudness = loudness * one(*cut)
    return loudness


def profile(amount, total, bound, lean):
    loads = [(1 << 20) // math.isqrt(rank ** lean) + 1 for rank in range(2, amount + 1)]
    rest, given = total - bound - (amount - 1), [1] * (amount - 1)
    while rest > 0:
        candidates = [i for i in range(amount - 1) if given[i] < bound]
        pool, remaining = sum([loads[i] for i in candidates]), rest
        for i in candidates:
            addition = min(bound - given[i], max(1, remaining * loads[i] // pool), rest)
            given[i] = given[i] + addition
            rest = rest - addition
    return np.array([bound] + given)


def ragged_sizes(key, amount, total, most, lean):
    if amount == 2:
        one = jax.random.randint(key, (), max(1, total - most), min(most, total - 1) + 1)
        return jnp.stack([one, total - one])
    sizes = jnp.asarray(profile(amount, total, most, lean), jnp.int32)
    twos = (amount - 1) // 2
    donor, sink = sizes[1:1 + 2 * twos:2], sizes[2:2 + 2 * twos:2]
    room = jnp.minimum(donor - 1, most - sink)
    passed = jax.random.randint(jax.random.fold_in(key, 1), (twos,), 0, 1 << 20) % (room + 1)
    sizes = sizes.at[1:1 + 2 * twos:2].set(donor - passed).at[2:2 + 2 * twos:2].set(sink + passed)
    return sizes[jax.random.permutation(jax.random.fold_in(key, 2), amount)]


def gaussian(stream_key, shape, deviation, bound, split=(), held_as=jnp.bfloat16):
    values = deviation * jax.random.normal(stream_key, shape, jnp.float32)
    if split:
        values = values * steps_of(stream_key, shape, split, -0.22, 0.18)
    return jnp.clip(values, -bound, bound).astype(held_as)


def setup_inputs(seed: int = 0) -> dict:
    key_of = jax.random.split(jax.random.key(seed), 7)
    return {
        "observations": gaussian(key_of[0], (STEPS, SITES), 8.0, 48.0, ((0, 32),), jnp.float32),
        "site_ids": with_ends(jax.random.randint(key_of[1], (STEPS, SITES), 0, GRID), jax.random.fold_in(key_of[1], 1), 0, GRID - 1).astype(jnp.int32),
        "counts": ragged_sizes(key_of[2], STEPS, STEPS * SITES * 3 // 4, SITES, 0).astype(jnp.int32),
        "frequencies": jnp.clip(jax.random.uniform(key_of[3], (MODES,), jnp.float32, -3.140625, 3.140625), -3.140625, 3.140625),
        "decay": jnp.clip(jnp.exp(jax.random.uniform(key_of[4], (MODES,), jnp.float32, math.log(0.02), math.log(0.2))), 0.02, 0.2),
        "proc_var": jnp.clip(jnp.exp(jax.random.uniform(key_of[5], (MODES,), jnp.float32, math.log(0.05), math.log(0.2))), 0.05, 0.2),
    }


exact_mode = lax.Precision.HIGHEST

def product(left, right):
    return jnp.dot(left.astype(jnp.float32), right.astype(jnp.float32), precision=exact_mode, preferred_element_type=jnp.float32)

def rotate_rows(matrix, damping, cosines, sines, backward):
    width = matrix.shape[0]
    pairs = matrix.reshape((width // 2, 2) + matrix.shape[1:])
    expand = (width // 2,) + (1,) * (matrix.ndim - 1)
    damp_part = damping.reshape(expand)
    cos_part = cosines.reshape(expand)
    sin_part = sines.reshape(expand)
    upper = pairs[:, 0]
    lower = pairs[:, 1]
    if backward:
        new_upper = damp_part * (cos_part * upper + sin_part * lower)
        new_lower = damp_part * (cos_part * lower - sin_part * upper)
    else:
        new_upper = damp_part * (cos_part * upper - sin_part * lower)
        new_lower = damp_part * (sin_part * upper + cos_part * lower)
    return jnp.stack([new_upper, new_lower], axis=1).reshape(matrix.shape)

def rotate_cols(matrix, damping, cosines, sines, transposed):
    return rotate_rows(matrix.T, damping, cosines, sines, not transposed).T

def site_features(site_row, live, modes):
    slots = jnp.arange(site_row.shape[0], dtype=jnp.int32)
    weights = (slots < live).astype(jnp.float32)
    orders = jnp.arange(1, modes + 1, dtype=jnp.int32)
    phase = site_row[:, None] * orders[None, :] % GRID
    angles = phase.astype(jnp.float32) * (2.0 * math.pi / GRID)
    features = jnp.stack([jnp.cos(angles), jnp.sin(angles)], axis=-1)
    features = features.reshape(site_row.shape[0], 2 * modes) * (1.0 / math.sqrt(modes))
    return (features, weights)

def gram(weighted, features):
    return lax.dot_general(weighted.astype(jnp.float32), features.astype(jnp.float32), (((0,), (0,)), ((), ())), precision=exact_mode, preferred_element_type=jnp.float32)

def build_element(precision_obs, info_obs, first, damping, cosines, sines, proc_var):
    per_mode = jnp.where(first, (1.0 - damping * damping) / proc_var, 1.0 / proc_var)
    diag_prec = jnp.repeat(per_mode, 2)
    keep = jnp.where(first, 0.0, 1.0).astype(jnp.float32)
    width = diag_prec.shape[0]
    factor = jnp.linalg.cholesky(jnp.diag(diag_prec) + precision_obs)
    covariance = jax.scipy.linalg.cho_solve((factor, True), jnp.eye(width, dtype=jnp.float32))
    shift_vec = product(covariance, info_obs)
    trans = rotate_cols(covariance * diag_prec[None, :], damping, cosines, sines, False) * keep
    inner_mat = jnp.diag(diag_prec) - diag_prec[:, None] * covariance * diag_prec[None, :]
    prec_mat = rotate_cols(rotate_rows(inner_mat, damping, cosines, sines, True), damping, cosines, sines, False) * keep
    info_vec = rotate_rows(diag_prec * shift_vec, damping, cosines, sines, True) * keep
    return (trans, shift_vec, covariance, info_vec, prec_mat)

def combine(earlier, later):
    a_trans, a_shift, a_cov, a_info, a_prec = earlier
    b_trans, b_shift, b_cov, b_info, b_prec = later
    width = a_cov.shape[0]
    factor = jnp.linalg.cholesky(a_cov)
    inner_mat = jnp.eye(width, dtype=jnp.float32) + product(product(factor.T, b_prec), factor)
    inner_fac = jnp.linalg.cholesky(inner_mat)
    solved = jax.scipy.linalg.cho_solve((inner_fac, True), product(factor.T, b_trans.T)).T
    gain_cov = product(solved, factor.T)
    gain_dyn = b_trans - product(gain_cov, b_prec)
    new_trans = product(gain_dyn, a_trans)
    new_shift = product(gain_dyn, a_shift) + product(gain_cov, b_info) + b_shift
    new_cov = product(gain_cov, b_trans.T) + b_cov
    back_prec = product(a_trans.T, b_prec)
    weight_solve = jax.scipy.linalg.cho_solve((inner_fac, True), product(factor.T, back_prec.T)).T
    weight_cov = product(weight_solve, factor.T)
    back_map = a_trans.T - weight_cov
    back_full = back_prec - product(weight_cov, b_prec)
    new_info = product(back_map, b_info) - product(back_full, a_shift) + a_info
    new_prec = product(back_full, a_trans) + a_prec
    return (new_trans, new_shift, new_cov, new_info, new_prec)

def smooth_element(mean, covariance, last, damping, cosines, sines, proc_var):
    keep = jnp.where(last, 0.0, 1.0).astype(jnp.float32)
    forward_cov = rotate_rows(covariance, damping, cosines, sines, False)
    predicted = rotate_cols(forward_cov, damping, cosines, sines, True) + jnp.diag(jnp.repeat(proc_var, 2))
    gain = jax.scipy.linalg.cho_solve((jnp.linalg.cholesky(predicted), True), forward_cov).T
    moved_mean = rotate_rows(mean, damping, cosines, sines, False)
    smooth_shift = mean - keep * product(gain, moved_mean)
    smooth_rest = covariance - keep * product(gain, forward_cov)
    return (gain * keep, smooth_shift, smooth_rest)

def smooth_combine(earlier, later):
    a_gain, a_shift, a_rest = earlier
    b_gain, b_shift, b_rest = later
    return (product(a_gain, b_gain), product(a_gain, b_shift) + a_shift, product(product(a_gain, b_rest), a_gain.T) + a_rest)

def reference(observations, site_ids, counts, frequencies, decay, proc_var):
    damping = jnp.exp(-decay)
    cosines = jnp.cos(frequencies)
    sines = jnp.sin(frequencies)
    modes = frequencies.shape[0]
    total = observations.shape[0]
    indices = jnp.arange(total, dtype=jnp.int32)
    noise_scale = 1.0 / OBS_VAR

    def element_at(packed):
        site_row, obs_row, live, index = packed
        features, weights = site_features(site_row, live, modes)
        weighted = features * weights[:, None]
        precision_obs = gram(weighted, features) * noise_scale
        info_obs = jnp.dot((obs_row * weights).astype(jnp.float32), features.astype(jnp.float32), precision=exact_mode, preferred_element_type=jnp.float32) * noise_scale
        return build_element(precision_obs, info_obs, index == 0, damping, cosines, sines, proc_var)
    elements = lax.map(element_at, (site_ids, observations, counts, indices))
    head = jax.tree.map(lambda whole: whole[0], elements)
    others = jax.tree.map(lambda whole: whole[1:], elements)

    def forward(carry, element):
        merged = combine(carry, element)
        return (merged, (merged[1], merged[2]))
    _, (means_rest, covs_rest) = lax.scan(forward, head, others)
    means = jnp.concatenate([head[1][None], means_rest], axis=0)
    covs = jnp.concatenate([head[2][None], covs_rest], axis=0)

    def smooth_at(packed):
        mean, covariance, index = packed
        return smooth_element(mean, covariance, index == total - 1, damping, cosines, sines, proc_var)
    smoothing = lax.map(smooth_at, (means, covs, indices))
    tail = jax.tree.map(lambda whole: whole[-1], smoothing)
    before = jax.tree.map(lambda whole: whole[:-1], smoothing)

    def backward(carry, element):
        merged = smooth_combine(element, carry)
        return (merged, (merged[1], merged[2]))
    _, (shift_rest, rest_rest) = lax.scan(backward, tail, before, reverse=True)
    smooth_mean = jnp.concatenate([shift_rest, tail[1][None]], axis=0)
    smooth_cov = jnp.concatenate([rest_rest, tail[2][None]], axis=0)
    return (smooth_mean, smooth_cov)
```

```python
import math

import jax
import jax.numpy as jnp
import numpy as np
from jax import lax
from jax.experimental import pallas as pl
from jax.experimental.pallas import tpu as pltpu
from jax.sharding import PartitionSpec as P

GRID = 4096
OBS_VAR = 64
MODES = 128
WIDTH = 2 * MODES
LOW = 32
HIGH = GRID // LOW
CHAIN_LIMIT = 1e-4
FINAL_LIMIT = 1e-2
NEWTON_STEPS = 30

NN = (((1,), (0,)), ((), ()))
NT = (((1,), (1,)), ((), ()))


def tables():
    order = np.arange(MODES, dtype=np.int64)
    high = np.arange(HIGH, dtype=np.int64)
    low = np.arange(LOW, dtype=np.int64)
    turn = 2.0 * math.pi * ((high[:, None] * order[None, :]) % HIGH) / HIGH
    transform = np.concatenate([np.cos(turn), np.sin(turn)], axis=1)
    reverse = MODES - order
    reverse[0] = 2 * MODES
    twiddles = []
    for multiples in (order, order + MODES, reverse, order + 1):
        turn = 2.0 * math.pi * ((low[:, None] * multiples[None, :]) % GRID) / GRID
        twiddles += [np.cos(turn), np.sin(turn)]
    return transform.astype(np.float32), np.stack(twiddles).astype(np.float32)


def dot(left, right, dims=NN):
    return lax.dot_general(left, right, dims, preferred_element_type=jnp.float32)


def exact_dot(left, right, dims=None):
    dims = dims or (((1,), (0,)), ((), ()))
    return lax.dot_general(
        left, right, dims, precision=lax.Precision.HIGHEST, preferred_element_type=jnp.float32
    )


def rounded(array):
    return array.astype(jnp.bfloat16)


def split(array):
    upper = rounded(array)
    return upper, rounded(array - upper.astype(jnp.float32))


def dot3(left, right, dims=NN):
    a_hi, a_lo = left
    b_hi, b_lo = right
    return dot(a_hi, b_hi, dims) + (dot(a_hi, b_lo, dims) + dot(a_lo, b_hi, dims))


def iota(shape, dim):
    return lax.broadcasted_iota(jnp.int32, shape, dim)


def statistics_kernel(count_ref, site_ref, obs_ref, transform_ref, twiddle_ref, out_ref):
    sites = site_ref.shape[1]
    site = site_ref[...]
    live = iota((1, sites), 1) < count_ref[0]
    low = jnp.where(live, site & (LOW - 1), LOW)
    high = site >> (LOW.bit_length() - 1)
    obs = obs_ref[...]
    first = rounded(obs).astype(jnp.float32)
    second = rounded(obs - first).astype(jnp.float32)
    third = obs - first - second
    here = iota((LOW, sites), 0) == low
    zero = jnp.zeros((LOW, sites), jnp.float32)
    stack = jnp.concatenate(
        [
            jnp.where(here, 1.0, zero),
            jnp.where(here, first, zero),
            jnp.where(here, second, zero),
            jnp.where(here, third, zero),
        ],
        axis=0,
    )
    columns = jnp.where(iota((HIGH, sites), 0) == high, 1.0, 0.0)
    binned = dot(rounded(stack), rounded(columns), NT)
    observed = binned[LOW : 2 * LOW] + binned[2 * LOW : 3 * LOW] + binned[3 * LOW :]
    waves = exact_dot(jnp.concatenate([binned[:LOW], observed], axis=0), transform_ref[...])
    real, imag = waves[:LOW, :MODES], waves[:LOW, MODES:]
    real_obs = pltpu.roll(waves[LOW:, :MODES], MODES - 1, 1)
    imag_obs = pltpu.roll(waves[LOW:, MODES:], MODES - 1, 1)
    sources = ((real, imag), (real, imag), (real, -imag), (real_obs, imag_obs))
    for kind, (re, im) in enumerate(sources):
        cosine, sine = twiddle_ref[2 * kind], twiddle_ref[2 * kind + 1]
        out_ref[2 * kind : 2 * kind + 1, :] = jnp.sum(re * cosine - im * sine, 0, keepdims=True)
        out_ref[2 * kind + 1 : 2 * kind + 2, :] = jnp.sum(
            re * sine + im * cosine, 0, keepdims=True
        )


def shear(rows, left):
    row = iota((8, MODES), 0)
    value = jnp.broadcast_to(rows, (8, MODES))
    for bit in (1, 2, 4):
        value = jnp.where((row & bit) != 0, pltpu.roll(value, MODES - bit if left else bit, 1), value)
    return value


def turned(value, amount):
    amount = amount % MODES
    return value if amount == 0 else pltpu.roll(value, amount, 1)


def build_block(stats, phase, block_ref):
    lane_row = iota((1, MODES), 1)
    u_re, u_im = phase[0:1], phase[1:2]
    columns = phase.T
    c_re, c_im = columns[:, 0:1], columns[:, 1:2]
    ahead = [pltpu.roll(stats[i : i + 1], MODES - 2, 1) for i in range(6)]
    inside = lane_row < MODES - 2
    t_re = (shear(stats[0:1], False), shear(stats[4:5], False))
    t_im = (shear(-stats[1:2], False), shear(stats[5:6], False))
    h_re = (
        shear(jnp.where(inside, ahead[0], ahead[2]), True),
        shear(jnp.where(inside, ahead[2], ahead[4]), True),
    )
    h_im = (
        shear(jnp.where(inside, ahead[1], ahead[3]), True),
        shear(jnp.where(inside, ahead[3], ahead[5]), True),
    )
    row, lane = iota((8, MODES), 0), iota((8, MODES), 1)
    for group in range(MODES // 8):
        start = 8 * group
        near = (lane >= row) & (lane < MODES - start)
        tr = turned(jnp.where(near, *t_re), start)
        ti = turned(jnp.where(near, *t_im), start)
        near = (lane >= start) & (lane + row < MODES)
        hr = turned(jnp.where(near, *h_re), -start)
        hi = turned(jnp.where(near, *h_im), -start)
        a_re, a_im = tr * u_re + ti * u_im, ti * u_re - tr * u_im
        b_re, b_im = hr * u_re - hi * u_im, hi * u_re + hr * u_im
        p_re, p_im, m_re, m_im = a_re + b_re, a_im + b_im, a_re - b_re, a_im - b_im
        cr, ci = c_re[start : start + 8], c_im[start : start + 8]
        block_ref[start : start + 8, :MODES] = cr * p_re - ci * p_im
        block_ref[start : start + 8, MODES:] = -(cr * m_im + ci * m_re)
        block_ref[MODES + start : MODES + start + 8, :MODES] = cr * p_im + ci * p_re
        block_ref[MODES + start : MODES + start + 8, MODES:] = cr * m_re - ci * m_im
    scale = MODES / (OBS_VAR * math.sqrt(MODES))
    o_re, o_im = stats[6:7] * scale, stats[7:8] * scale
    return jnp.concatenate([o_re * u_re - o_im * u_im, o_re * u_im + o_im * u_re], axis=1)


def diagonal_mask():
    shape = (MODES, MODES)
    return jnp.where(iota(shape, 0) == iota(shape, 1), 1.0, 0.0)


def spread(row, mask):
    zero = jnp.zeros((MODES, MODES), jnp.float32)
    upper = jnp.concatenate([mask * row[:, :MODES], zero], axis=1)
    return jnp.concatenate([upper, jnp.concatenate([zero, mask * row[:, MODES:]], axis=1)], axis=0)


def diagonal_of(matrix, mask, axis):
    upper = jnp.sum(matrix[:MODES, :MODES] * mask, axis=axis, keepdims=True)
    lower = jnp.sum(matrix[MODES:, MODES:] * mask, axis=axis, keepdims=True)
    return jnp.concatenate([upper, lower], axis=1 - axis)


def off_diagonal(matrix, mask):
    other = 1.0 - mask
    upper = jnp.concatenate([matrix[:MODES, :MODES] * other, matrix[:MODES, MODES:]], axis=1)
    lower = jnp.concatenate([matrix[MODES:, :MODES], matrix[MODES:, MODES:] * other], axis=1)
    return jnp.concatenate([upper, lower], axis=0)


def jacobi(excess, base, mask):
    by_row = lax.rsqrt(base[1] + diagonal_of(excess, mask, 1))
    own = diagonal_of(excess, mask, 0)
    by_lane = lax.rsqrt(base[0] + own)
    scale = by_row * by_lane
    return -off_diagonal(excess, mask) * scale, scale, by_lane, own


def squares(array):
    return jnp.sum(array * array, axis=0, keepdims=True)


def chain_inverse(excess, base, damping, mask):
    residue, scale, by_lane, own = jacobi(excess, base, mask)
    parts = split(residue)
    second = dot3(parts, parts)
    first_two = residue + second
    rest = (first_two + dot(rounded(second), rounded(first_two))) * scale
    diagonal = by_lane * by_lane
    lost = spread(damping[0] * own * diagonal, mask) - rest
    return rest, diagonal, lost, squares(second)


def final_inverse(excess, base, damping, mask):
    residue, scale, by_lane, _ = jacobi(excess, base, mask)
    parts = split(residue)
    second = dot3(parts, parts)
    second_hi = rounded(second)
    near = residue + second + dot(parts[0], second_hi)
    fourth = dot(second_hi, second_hi)
    rest = near + fourth + dot(rounded(near), rounded(fourth))
    return rest * scale, by_lane * by_lane, None, squares(second)


def final_rows(excess, base, rows, mask):
    residue, _, by_lane, _ = jacobi(excess, base, mask)
    parts = split(residue)
    second = dot3(parts, parts)
    second_parts = split(second)
    fourth = rounded(dot(second_parts[0], second_parts[0]))
    value = rows * by_lane
    value = value + dot3(split(value), parts)
    value = value + dot3(split(value), second_parts)
    value = value + dot(rounded(value), fourth)
    return value * by_lane, squares(second)


def product3(left, right, dims=NN):
    return dot3(split(left), split(right), dims)


def eliminate(carried, kept, rest, diagonal, mask, product):
    moved = carried * diagonal + product(carried, rest)
    return moved, moved * kept + product(moved, carried[:WIDTH] - spread(kept, mask), NT)


def solve_kernel(
    place_ref,
    stats_ref,
    frequency_ref,
    decay_ref,
    variance_ref,
    mean_ref,
    cov_ref,
    check_ref,
    phase_ref,
    block1_ref,
    block2_ref,
    rest1_ref,
    rest2_ref,
    lost1_ref,
    lost2_ref,
    saved_ref,
    far_ref,
    carried_ref,
    rows_ref,
    columns_ref,
):
    steps = stats_ref.shape[0]
    half = steps // 2
    time, shard = place_ref[0], place_ref[1]
    flip = time < half
    node = jnp.where(flip, steps - 1 - time, time)
    outer = steps - 1 - node

    def time_of(index):
        return jnp.where(flip, steps - 1 - index, index)

    decays = jnp.exp(-decay_ref[...])
    scale = jnp.sqrt(variance_ref[...] / decays)
    positions = iota((steps, MODES), 0)
    angles = time_of(positions).astype(jnp.float32) * frequency_ref[...]
    cosines = jnp.cos(angles) * (scale / MODES)
    sines = jnp.sin(angles) * (-scale / MODES)
    for index in range(steps):
        phase_ref[index, 0:1, :] = cosines[index : index + 1]
        phase_ref[index, 1:2, :] = sines[index : index + 1]
        phase_ref[index, 2:8, :] = jnp.zeros((6, MODES), jnp.float32)
    twice = jnp.concatenate([decays, decays], axis=1)
    own_base = (1.0 - twice * twice) / twice
    values = (twice, 1.0 / twice, own_base)
    table = jnp.concatenate(values + (jnp.zeros((5, WIDTH), jnp.float32),), axis=0)
    columns_ref[:MODES] = table[:, :MODES].T
    columns_ref[MODES:] = table[:, MODES:].T
    damping, base, own_base = (
        (value, columns_ref[:, i : i + 1]) for i, value in enumerate(values)
    )

    def build(index, block_ref):
        return build_block(stats_ref[time_of(index)], phase_ref[index], block_ref)

    def second_node(index):
        late = jnp.where(index >= half - 1, node, half + index - outer)
        return jnp.where(index < outer, steps - 1 - index, late)

    def run(invert_chain, invert_middle, finish, product):
        mask = diagonal_mask()
        for ref in (rest1_ref, rest2_ref, lost1_ref, lost2_ref, saved_ref, far_ref, carried_ref):
            ref[...] = jnp.zeros(ref.shape, jnp.float32)
        rows_ref[...] = jnp.zeros(rows_ref.shape, jnp.float32)
        check_ref[...] = jnp.zeros(check_ref.shape, jnp.float32)
        rows_ref[8:9, :] = build(0, block1_ref)
        rows_ref[16:17, :] = build(second_node(0), block2_ref)

        def advance(index):
            fresh = index == outer
            excess1 = block1_ref[...] + lost1_ref[...]
            lost2 = lost2_ref[...]
            saved_ref[...] = jnp.where(fresh, lost2, saved_ref[...])
            excess2 = block2_ref[...] + jnp.where(fresh, spread(damping[0], mask), lost2)
            diagonal1, diagonal2 = rows_ref[32:33, :], rows_ref[33:34, :]
            before = rows_ref[0:8, :]
            info1 = rows_ref[8:16, :] + before * diagonal1 + product(before, rest1_ref[...])
            kept = rows_ref[34:35, :]
            moved, left = eliminate(
                carried_ref[...], kept, rest2_ref[...], diagonal2, mask, product
            )
            info2 = moved[WIDTH:]
            rows_ref[34:35, :] = jnp.where(fresh, 1.0, kept * diagonal2)
            rows_ref[24:32, :] = jnp.where(fresh, info2, rows_ref[24:32, :])
            far_ref[...] = jnp.where(fresh, 0.0, far_ref[...] + left)
            ones = jnp.ones((1, WIDTH), jnp.float32)
            carried_ref[:WIDTH] = jnp.where(fresh, spread(ones, mask), moved[:WIDTH])
            info2 = jnp.where(fresh, 0.0, info2) + rows_ref[16:24, :]
            carried_ref[WIDTH:] = info2
            rows_ref[0:8, :] = info1
            return excess1, excess2, info1, info2

        def body(index, _):
            excess1, excess2, _, _ = advance(index)
            next1 = invert_chain(excess1, base, damping, mask)
            next2 = invert_chain(excess2, base, damping, mask)
            rest1_ref[...], rows_ref[32:33, :], lost1_ref[...] = next1
            rest2_ref[...], rows_ref[33:34, :], lost2_ref[...] = next2
            rows_ref[8:9, :] = build(index + 1, block1_ref)
            rows_ref[16:17, :] = build(second_node(index + 1), block2_ref)
            return 0

        lax.fori_loop(0, half - 1, body, 0)
        excess1, excess2, info1, info2 = advance(half - 1)
        rest, diagonal, _ = invert_middle(excess1 - far_ref[:WIDTH], base, damping, mask)
        carried_ref[:WIDTH] = carried_ref[:WIDTH].T
        carried_ref[WIDTH:] = info1 + far_ref[WIDTH:]
        _, left = eliminate(carried_ref[...], rows_ref[34:35, :], rest, diagonal, mask, product)
        excess = excess2 + saved_ref[...] - left[:WIDTH]
        info = info2 + rows_ref[24:32, :] + left[WIDTH:]

        block = cov_ref.shape[0]
        cosine = phase_ref[node, 0:1, :] * MODES
        sine = phase_ref[node, 1:2, :] * (-MODES)
        even = jnp.concatenate([cosine, -sine], axis=1)
        odd = jnp.concatenate([sine, cosine], axis=1)

        def turn_back(rows, start):
            row = iota((rows, WIDTH), 0) + start
            lane = iota((rows, WIDTH), 1) & (MODES - 1)
            value = jnp.where((row & 1) == 0, even, odd)
            return jnp.where(lane == (row >> 1), value, 0.0)

        mine = turn_back(block, shard * block)
        whole = split(turn_back(WIDTH, 0))
        (result,) = finish(excess, own_base, jnp.concatenate([mine, info], axis=0), mask)
        mean_ref[...] = dot3(split(result[block:]), split(mine), NT)[0:1]
        cov_ref[...] = dot3(split(result[:block]), whole, NT)

    def noted(inverse, row):
        def call(*args):
            *value, measure = inverse(*args)
            check_ref[row : row + 1, :] = jnp.maximum(check_ref[row : row + 1, :], measure)
            return value

        return call

    run(noted(chain_inverse, 0), noted(final_inverse, 1), noted(final_rows, 1), product3)


def solve(place, stats, frequencies, decay, proc_var, block):
    square = pltpu.VMEM((WIDTH, WIDTH), jnp.float32)
    tall = pltpu.VMEM((WIDTH + 8, WIDTH), jnp.float32)
    vmem = pl.BlockSpec(memory_space=pltpu.VMEM)
    return pl.pallas_call(
        solve_kernel,
        out_shape=(
            jax.ShapeDtypeStruct((1, block), jnp.float32),
            jax.ShapeDtypeStruct((block, WIDTH), jnp.float32),
            jax.ShapeDtypeStruct((2, WIDTH), jnp.float32),
        ),
        in_specs=[pl.BlockSpec(memory_space=pltpu.SMEM)] + [vmem] * 4,
        out_specs=(vmem, vmem, vmem),
        scratch_shapes=[
            pltpu.VMEM((stats.shape[0], 8, MODES), jnp.float32),
            *[square] * 7,
            tall,
            tall,
            pltpu.VMEM((40, WIDTH), jnp.float32),
            pltpu.VMEM((WIDTH, 8), jnp.float32),
        ],
        compiler_params=pltpu.CompilerParams(vmem_limit_bytes=48 << 20),
        name="solve",
    )(place, stats, frequencies[None], decay[None], proc_var[None])


def newton_inverse(matrix):
    eye = jnp.eye(WIDTH, dtype=jnp.float32)
    start = eye / jnp.sum(jnp.abs(matrix), axis=1, keepdims=True)

    def step(_, approx):
        return approx + exact_dot(approx, eye - exact_dot(matrix, approx))

    return lax.fori_loop(0, NEWTON_STEPS, step, start)


def general(place, stats, frequencies, decay, proc_var, block):
    steps = stats.shape[0]
    time, shard = place[0], place[1]
    damping = jnp.exp(-decay)
    scale = jnp.sqrt(proc_var / damping)
    twice = jnp.concatenate([damping, damping])
    order = jnp.arange(1, MODES + 1)
    apart, together = order[:, None] - order[None, :], order[:, None] + order[None, :]
    direction = jnp.sign(apart).astype(jnp.float32)

    def node(index):
        rows = stats[index]
        even = jnp.concatenate([rows[0], rows[2], rows[4, :1]])
        odd = jnp.concatenate([rows[1], rows[3], rows[5, :1]])
        angle = index.astype(jnp.float32) * frequencies
        u_re, u_im = scale / MODES * jnp.cos(angle), -scale / MODES * jnp.sin(angle)
        t_re, t_im = even[jnp.abs(apart)], direction * odd[jnp.abs(apart)]
        h_re, h_im = even[together], odd[together]
        a_re, a_im = t_re * u_re + t_im * u_im, t_im * u_re - t_re * u_im
        b_re, b_im = h_re * u_re - h_im * u_im, h_im * u_re + h_re * u_im
        c_re, c_im = u_re[:, None], u_im[:, None]
        p_re, p_im, m_re, m_im = a_re + b_re, a_im + b_im, a_re - b_re, a_im - b_im
        upper = jnp.concatenate([c_re * p_re - c_im * p_im, -(c_re * m_im + c_im * m_re)], axis=1)
        lower = jnp.concatenate([c_re * p_im + c_im * p_re, c_re * m_re - c_im * m_im], axis=1)
        factor = MODES / (OBS_VAR * math.sqrt(MODES))
        o_re, o_im = rows[6] * factor, rows[7] * factor
        info = jnp.concatenate([o_re * u_re - o_im * u_im, o_re * u_im + o_im * u_re])
        return jnp.concatenate([upper, lower], axis=0), info

    def passed(index, state):
        lost, message = state
        precision, info = node(index)
        excess = precision + lost
        inverse = newton_inverse(jnp.diag(1.0 / twice) + excess)
        lost = twice[:, None] * exact_dot(excess, inverse)
        return 0.5 * (lost + lost.T), exact_dot(inverse, info + message)

    start = (jnp.zeros((WIDTH, WIDTH), jnp.float32), jnp.zeros((WIDTH,), jnp.float32))
    before = lax.fori_loop(0, time, passed, start)
    after = lax.fori_loop(
        0, steps - 1 - time, lambda index, state: passed(steps - 1 - index, state), start
    )
    precision, info = node(time)
    base = jnp.diag((1.0 - twice * twice) / twice)
    inverse = newton_inverse(base + precision + before[0] + after[0])
    angle = time.astype(jnp.float32) * frequencies
    cosine, sine = jnp.diag(scale * jnp.cos(angle)), jnp.diag(scale * jnp.sin(angle))
    back = jnp.stack(
        [jnp.concatenate([cosine, -sine], axis=1), jnp.concatenate([sine, cosine], axis=1)], axis=1
    ).reshape(WIDTH, WIDTH)
    mine = exact_dot(lax.dynamic_slice_in_dim(back, shard * block, block, 0), inverse)
    mean = exact_dot(mine, info + before[1] + after[1])
    return mean[None], exact_dot(mine, back, NT)


def statistics(site_row, obs_row, count):
    transform, twiddles = tables()
    vmem = pl.BlockSpec(memory_space=pltpu.VMEM)
    return pl.pallas_call(
        statistics_kernel,
        out_shape=jax.ShapeDtypeStruct((8, MODES), jnp.float32),
        in_specs=[pl.BlockSpec(memory_space=pltpu.SMEM)] + [vmem] * 4,
        out_specs=vmem,
        name="statistics",
    )(count, site_row, obs_row, jnp.asarray(transform), jnp.asarray(twiddles))


def local(observations, site_ids, counts, frequencies, decay, proc_var):
    steps = lax.axis_size("tm")
    block = WIDTH // lax.axis_size("rows")
    stats = statistics(site_ids, observations, counts)
    copies = jnp.broadcast_to(stats, (steps, *stats.shape))
    everyone = lax.all_to_all(copies, "tm", split_axis=0, concat_axis=0, tiled=True)
    place = jnp.stack([lax.axis_index("tm"), lax.axis_index("rows")]).astype(jnp.int32)
    mean, cov, check = solve(place, everyone, frequencies, decay, proc_var, block)
    measure = jnp.sum(check, axis=1)
    mean, cov = lax.cond(
        (measure[0] <= CHAIN_LIMIT) & (measure[1] <= FINAL_LIMIT),
        lambda place, everyone, mean, cov: (mean, cov),
        lambda place, everyone, mean, cov: general(
            place, everyone, frequencies, decay, proc_var, block
        ),
        place,
        everyone,
        mean,
        cov,
    )
    return mean, cov[None]


def solution(mesh):
    return jax.shard_map(
        local,
        mesh=mesh,
        in_specs=(P("tm", None), P("tm", None), P("tm"), P(), P(), P()),
        out_specs=(P("tm", "rows"), P("tm", "rows", None)),
        check_vma=False,
    )
```

```python
import math

import jax
import jax.numpy as jnp
import numpy as np
from jax import lax
from jax.experimental import pallas as pl
from jax.experimental.pallas import tpu as pltpu
from jax.sharding import PartitionSpec as P

GRID = 4096
OBS_VAR = 64
MODES = 128
WIDTH = 2 * MODES
LOW = 32
HIGH = GRID // LOW
CHAIN_LIMIT = 1e-4
FINAL_LIMIT = 1e-2
NEWTON_STEPS = 30

NN = (((1,), (0,)), ((), ()))
NT = (((1,), (1,)), ((), ()))


def tables():
    order = np.arange(MODES, dtype=np.int64)
    high = np.arange(HIGH, dtype=np.int64)
    low = np.arange(LOW, dtype=np.int64)
    turn = 2.0 * math.pi * ((high[:, None] * order[None, :]) % HIGH) / HIGH
    transform = np.concatenate([np.cos(turn), np.sin(turn)], axis=1)
    far_back = 2 * MODES + 1 - order
    far_back[0] = MODES + 1
    twiddles = []
    for multiples in (order, far_back, MODES - order, order + 1):
        turn = 2.0 * math.pi * ((low[:, None] * multiples[None, :]) % GRID) / GRID
        twiddles += [np.cos(turn), np.sin(turn)]
    return transform.astype(np.float32), np.stack(twiddles).astype(np.float32)


def dot(left, right, dims=NN):
    return lax.dot_general(left, right, dims, preferred_element_type=jnp.float32)


def exact_dot(left, right, dims=None):
    dims = dims or (((1,), (0,)), ((), ()))
    return lax.dot_general(
        left, right, dims, precision=lax.Precision.HIGHEST, preferred_element_type=jnp.float32
    )


def rounded(array):
    return array.astype(jnp.bfloat16)


def split(array):
    upper = rounded(array)
    return upper, rounded(array - upper.astype(jnp.float32))


def dot3(left, right, dims=NN):
    a_hi, a_lo = left
    b_hi, b_lo = right
    (left_dim,), (right_dim,) = dims[0]
    return dot(
        jnp.concatenate([a_hi, a_hi, a_lo], axis=left_dim),
        jnp.concatenate([b_hi, b_lo, b_hi], axis=right_dim),
        dims,
    )


def iota(shape, dim):
    return lax.broadcasted_iota(jnp.int32, shape, dim)


def statistics_kernel(count_ref, site_ref, obs_ref, transform_ref, twiddle_ref, out_ref):
    sites = site_ref.shape[1]
    site = site_ref[...]
    live = iota((1, sites), 1) < count_ref[0]
    low = jnp.where(live, site & (LOW - 1), LOW)
    high = site >> (LOW.bit_length() - 1)
    obs = obs_ref[...]
    first = rounded(obs).astype(jnp.float32)
    second = rounded(obs - first).astype(jnp.float32)
    third = obs - first - second
    here = iota((LOW, sites), 0) == low
    zero = jnp.zeros((LOW, sites), jnp.float32)
    stack = jnp.concatenate(
        [
            jnp.where(here, 1.0, zero),
            jnp.where(here, first, zero),
            jnp.where(here, second, zero),
            jnp.where(here, third, zero),
        ],
        axis=0,
    )
    columns = jnp.where(iota((HIGH, sites), 0) == high, 1.0, 0.0)
    binned = dot(rounded(stack), rounded(columns), NT)
    observed = binned[LOW : 2 * LOW] + binned[2 * LOW : 3 * LOW] + binned[3 * LOW :]
    waves = exact_dot(jnp.concatenate([binned[:LOW], observed], axis=0), transform_ref[...])
    real, imag = waves[:LOW, :MODES], waves[:LOW, MODES:]
    real_obs = pltpu.roll(waves[LOW:, :MODES], MODES - 1, 1)
    imag_obs = pltpu.roll(waves[LOW:, MODES:], MODES - 1, 1)
    turned = (pltpu.roll(real, 1, 1), pltpu.roll(-imag, 1, 1))
    sources = ((real, imag), turned, (real, -imag), (real_obs, imag_obs))
    for kind, (re, im) in enumerate(sources):
        cosine, sine = twiddle_ref[2 * kind], twiddle_ref[2 * kind + 1]
        out_ref[2 * kind : 2 * kind + 1, :] = jnp.sum(re * cosine - im * sine, 0, keepdims=True)
        out_ref[2 * kind + 1 : 2 * kind + 2, :] = jnp.sum(
            re * sine + im * cosine, 0, keepdims=True
        )


def toeplitz(ahead, behind):
    shape = (MODES, MODES)
    upper = pltpu.roll(jnp.broadcast_to(ahead, shape), 0, 1, stride=1, stride_axis=0)
    lower = pltpu.roll(jnp.broadcast_to(behind, shape), 0, 1, stride=1, stride_axis=0)
    return jnp.where(iota(shape, 1) >= iota(shape, 0), upper, lower)


def build_block(stats, phase, block_ref):
    u_re, u_im = phase[0:1], phase[1:2]
    columns = phase.T
    cr, ci = columns[:, 0:1], columns[:, 1:2]
    tr = toeplitz(stats[0:1], stats[4:5])
    ti = toeplitz(-stats[1:2], stats[5:6])
    start = iota((1, MODES), 1) == 0
    near = [
        jnp.where(start, stats[2 + i : 3 + i], pltpu.roll(stats[4 + i : 5 + i], 1, 1))
        for i in range(2)
    ]
    mirrored = jnp.concatenate(
        [toeplitz(near[0], stats[2:3]), toeplitz(near[1], stats[3:4])], axis=0
    )
    shape = (2 * MODES, MODES)
    row = iota(shape, 0) & (MODES - 1)
    mirror = rounded(jnp.where(row + iota(shape, 1) == MODES - 1, 1.0, 0.0))
    sums = dot(jnp.concatenate(split(mirrored), axis=1), mirror)
    hr, hi = sums[:MODES], sums[MODES:]
    a_re, a_im = tr * u_re + ti * u_im, ti * u_re - tr * u_im
    b_re, b_im = hr * u_re - hi * u_im, hi * u_re + hr * u_im
    p_re, p_im, m_re, m_im = a_re + b_re, a_im + b_im, a_re - b_re, a_im - b_im
    block_ref[:MODES, :MODES] = cr * p_re - ci * p_im
    block_ref[:MODES, MODES:] = -(cr * m_im + ci * m_re)
    block_ref[MODES:, :MODES] = cr * p_im + ci * p_re
    block_ref[MODES:, MODES:] = cr * m_re - ci * m_im
    scale = MODES / (OBS_VAR * math.sqrt(MODES))
    o_re, o_im = stats[6:7] * scale, stats[7:8] * scale
    return jnp.concatenate([o_re * u_re - o_im * u_im, o_re * u_im + o_im * u_re], axis=1)


def diagonal_mask():
    shape = (MODES, MODES)
    return jnp.where(iota(shape, 0) == iota(shape, 1), 1.0, 0.0)


def spread(row, mask):
    zero = jnp.zeros((MODES, MODES), jnp.float32)
    upper = jnp.concatenate([mask * row[:, :MODES], zero], axis=1)
    return jnp.concatenate([upper, jnp.concatenate([zero, mask * row[:, MODES:]], axis=1)], axis=0)


def diagonal_of(matrix, mask, axis):
    upper = jnp.sum(matrix[:MODES, :MODES] * mask, axis=axis, keepdims=True)
    lower = jnp.sum(matrix[MODES:, MODES:] * mask, axis=axis, keepdims=True)
    return jnp.concatenate([upper, lower], axis=1 - axis)


def off_diagonal(matrix, mask):
    other = 1.0 - mask
    upper = jnp.concatenate([matrix[:MODES, :MODES] * other, matrix[:MODES, MODES:]], axis=1)
    lower = jnp.concatenate([matrix[MODES:, :MODES], matrix[MODES:, MODES:] * other], axis=1)
    return jnp.concatenate([upper, lower], axis=0)


def jacobi(excess, base, mask):
    by_row = lax.rsqrt(base[1] + diagonal_of(excess, mask, 1))
    own = diagonal_of(excess, mask, 0)
    by_lane = lax.rsqrt(base[0] + own)
    scale = by_row * by_lane
    return -off_diagonal(excess, mask) * scale, scale, by_lane, own


def squares(array):
    return jnp.sum(array * array, axis=0, keepdims=True)


def chain_inverse(excess, base, damping, mask):
    residue, scale, by_lane, own = jacobi(excess, base, mask)
    parts = split(residue)
    second = dot3(parts, parts)
    first_two = residue + second
    rest = (first_two + dot(rounded(second), rounded(first_two))) * scale
    diagonal = by_lane * by_lane
    lost = spread(damping[0] * own * diagonal, mask) - rest
    return rest, diagonal, lost, squares(second)


def final_inverse(excess, base, damping, mask):
    residue, scale, by_lane, _ = jacobi(excess, base, mask)
    parts = split(residue)
    second = dot3(parts, parts)
    second_hi = rounded(second)
    near = residue + second + dot(parts[0], second_hi)
    fourth = dot(second_hi, second_hi)
    rest = near + fourth + dot(rounded(near), rounded(fourth))
    return rest * scale, by_lane * by_lane, None, squares(second)


def final_rows(excess, base, rows, mask):
    residue, _, by_lane, _ = jacobi(excess, base, mask)
    parts = split(residue)
    second = dot3(parts, parts)
    second_parts = split(second)
    fourth = rounded(dot(second_parts[0], second_parts[0]))
    value = rows * by_lane
    value = value + dot3(split(value), parts)
    value = value + dot3(split(value), second_parts)
    value = value + dot(rounded(value), fourth)
    return value * by_lane, squares(second)


def product3(left, right, dims=NN):
    return dot3(split(left), split(right), dims)


def eliminate(carried, kept, rest, diagonal, mask, product):
    moved = carried * diagonal + product(carried, rest)
    return moved, moved * kept + product(moved, carried[:WIDTH] - spread(kept, mask), NT)


def solve_kernel(
    place_ref,
    stats_ref,
    frequency_ref,
    decay_ref,
    variance_ref,
    mean_ref,
    cov_ref,
    check_ref,
    phase_ref,
    block1_ref,
    block2_ref,
    rest1_ref,
    rest2_ref,
    lost1_ref,
    lost2_ref,
    saved_ref,
    far_ref,
    carried_ref,
    rows_ref,
    columns_ref,
):
    steps = stats_ref.shape[0]
    half = steps // 2
    time, shard = place_ref[0], place_ref[1]
    flip = time < half
    node = jnp.where(flip, steps - 1 - time, time)
    outer = steps - 1 - node

    def time_of(index):
        return jnp.where(flip, steps - 1 - index, index)

    decays = jnp.exp(-decay_ref[...])
    scale = jnp.sqrt(variance_ref[...] / decays)
    positions = iota((steps, MODES), 0)
    angles = time_of(positions).astype(jnp.float32) * frequency_ref[...]
    cosines = jnp.cos(angles) * (scale / MODES)
    sines = jnp.sin(angles) * (-scale / MODES)
    for index in range(steps):
        phase_ref[index, 0:1, :] = cosines[index : index + 1]
        phase_ref[index, 1:2, :] = sines[index : index + 1]
        phase_ref[index, 2:8, :] = jnp.zeros((6, MODES), jnp.float32)
    twice = jnp.concatenate([decays, decays], axis=1)
    own_base = (1.0 - twice * twice) / twice
    values = (twice, 1.0 / twice, own_base)
    table = jnp.concatenate(values + (jnp.zeros((5, WIDTH), jnp.float32),), axis=0)
    columns_ref[:MODES] = table[:, :MODES].T
    columns_ref[MODES:] = table[:, MODES:].T
    damping, base, own_base = (
        (value, columns_ref[:, i : i + 1]) for i, value in enumerate(values)
    )

    def build(index, block_ref):
        return build_block(stats_ref[time_of(index)], phase_ref[index], block_ref)

    def second_node(index):
        late = jnp.where(index >= half - 1, node, half + index - outer)
        return jnp.where(index < outer, steps - 1 - index, late)

    def run(invert_chain, invert_middle, finish, product):
        mask = diagonal_mask()
        ones = jnp.ones((1, WIDTH), jnp.float32)
        for ref in (rest1_ref, rest2_ref, lost1_ref, lost2_ref, saved_ref, far_ref, carried_ref):
            ref[...] = jnp.zeros(ref.shape, jnp.float32)
        rows_ref[...] = jnp.zeros(rows_ref.shape, jnp.float32)
        check_ref[...] = jnp.zeros(check_ref.shape, jnp.float32)
        rows_ref[8:9, :] = build(0, block1_ref)
        rows_ref[16:17, :] = build(second_node(0), block2_ref)

        def advance(index):
            @pl.when(index == outer)
            def _():
                message = carried_ref[WIDTH:]
                saved_ref[...] = lost2_ref[...]
                rows_ref[24:32, :] = message * rows_ref[33:34, :] + product(message, rest2_ref[...])
                eye = spread(ones, mask)
                lost2_ref[...] = spread(damping[0], mask)
                rest2_ref[...] = jnp.zeros((WIDTH, WIDTH), jnp.float32)
                rows_ref[33:35, :] = jnp.ones((2, WIDTH), jnp.float32)
                carried_ref[:WIDTH] = eye
                carried_ref[WIDTH:] = jnp.zeros((8, WIDTH), jnp.float32)
                far_ref[:WIDTH] = -eye
                far_ref[WIDTH:] = jnp.zeros((8, WIDTH), jnp.float32)

            excess1 = block1_ref[...] + lost1_ref[...]
            excess2 = block2_ref[...] + lost2_ref[...]
            diagonal1, diagonal2 = rows_ref[32:33, :], rows_ref[33:34, :]
            before = rows_ref[0:8, :]
            info1 = rows_ref[8:16, :] + before * diagonal1 + product(before, rest1_ref[...])
            kept = rows_ref[34:35, :]
            moved, left = eliminate(
                carried_ref[...], kept, rest2_ref[...], diagonal2, mask, product
            )
            rows_ref[34:35, :] = kept * diagonal2
            far_ref[...] += left
            carried_ref[:WIDTH] = moved[:WIDTH]
            info2 = moved[WIDTH:] + rows_ref[16:24, :]
            carried_ref[WIDTH:] = info2
            rows_ref[0:8, :] = info1
            return excess1, excess2, info1, info2

        def body(index, _):
            excess1, excess2, _, _ = advance(index)
            next1 = invert_chain(excess1, base, damping, mask)
            next2 = invert_chain(excess2, base, damping, mask)
            rest1_ref[...], rows_ref[32:33, :], lost1_ref[...] = next1
            rest2_ref[...], rows_ref[33:34, :], lost2_ref[...] = next2
            rows_ref[8:9, :] = build(index + 1, block1_ref)
            rows_ref[16:17, :] = build(second_node(index + 1), block2_ref)
            return 0

        lax.fori_loop(0, half - 1, body, 0)
        excess1, excess2, info1, info2 = advance(half - 1)
        rest, diagonal, _ = invert_middle(excess1 - far_ref[:WIDTH], base, damping, mask)
        carried_ref[:WIDTH] = carried_ref[:WIDTH].T
        carried_ref[WIDTH:] = info1 + far_ref[WIDTH:]
        _, left = eliminate(carried_ref[...], rows_ref[34:35, :], rest, diagonal, mask, product)
        excess = excess2 + saved_ref[...] - left[:WIDTH]
        info = info2 + rows_ref[24:32, :] + left[WIDTH:]

        block = cov_ref.shape[0]
        cosine = phase_ref[node, 0:1, :] * MODES
        sine = phase_ref[node, 1:2, :] * (-MODES)
        even = jnp.concatenate([cosine, -sine], axis=1)
        odd = jnp.concatenate([sine, cosine], axis=1)

        def turn_back(rows, start):
            row = iota((rows, WIDTH), 0) + start
            lane = iota((rows, WIDTH), 1) & (MODES - 1)
            value = jnp.where((row & 1) == 0, even, odd)
            return jnp.where(lane == (row >> 1), value, 0.0)

        mine = turn_back(block, shard * block)
        whole = split(turn_back(WIDTH, 0))
        (result,) = finish(excess, own_base, jnp.concatenate([mine, info], axis=0), mask)
        mean_ref[...] = dot3(split(result[block:]), split(mine), NT)[0:1]
        cov_ref[...] = dot3(split(result[:block]), whole, NT)

    def noted(inverse, row):
        def call(*args):
            *value, measure = inverse(*args)
            check_ref[row : row + 1, :] = jnp.maximum(check_ref[row : row + 1, :], measure)
            return value

        return call

    run(noted(chain_inverse, 0), noted(final_inverse, 1), noted(final_rows, 1), product3)


def solve(place, stats, frequencies, decay, proc_var, block):
    square = pltpu.VMEM((WIDTH, WIDTH), jnp.float32)
    tall = pltpu.VMEM((WIDTH + 8, WIDTH), jnp.float32)
    vmem = pl.BlockSpec(memory_space=pltpu.VMEM)
    return pl.pallas_call(
        solve_kernel,
        out_shape=(
            jax.ShapeDtypeStruct((1, block), jnp.float32),
            jax.ShapeDtypeStruct((block, WIDTH), jnp.float32),
            jax.ShapeDtypeStruct((2, WIDTH), jnp.float32),
        ),
        in_specs=[pl.BlockSpec(memory_space=pltpu.SMEM)] + [vmem] * 4,
        out_specs=(vmem, vmem, vmem),
        scratch_shapes=[
            pltpu.VMEM((stats.shape[0], 8, MODES), jnp.float32),
            *[square] * 7,
            tall,
            tall,
            pltpu.VMEM((40, WIDTH), jnp.float32),
            pltpu.VMEM((WIDTH, 8), jnp.float32),
        ],
        compiler_params=pltpu.CompilerParams(vmem_limit_bytes=48 << 20),
        name="solve",
    )(place, stats, frequencies[None], decay[None], proc_var[None])


def newton_inverse(matrix):
    eye = jnp.eye(WIDTH, dtype=jnp.float32)
    start = eye / jnp.sum(jnp.abs(matrix), axis=1, keepdims=True)

    def step(_, approx):
        return approx + exact_dot(approx, eye - exact_dot(matrix, approx))

    return lax.fori_loop(0, NEWTON_STEPS, step, start)


def general(place, stats, frequencies, decay, proc_var, block):
    steps = stats.shape[0]
    time, shard = place[0], place[1]
    damping = jnp.exp(-decay)
    scale = jnp.sqrt(proc_var / damping)
    twice = jnp.concatenate([damping, damping])
    order = jnp.arange(1, MODES + 1)
    apart, together = order[:, None] - order[None, :], order[:, None] + order[None, :]
    direction = jnp.sign(apart).astype(jnp.float32)

    def node(index):
        rows = stats[index]
        even = jnp.concatenate([rows[0], rows[4, :1], rows[2, :1], rows[2, :0:-1]])
        odd = jnp.concatenate([rows[1], rows[5, :1], rows[3, :1], rows[3, :0:-1]])
        angle = index.astype(jnp.float32) * frequencies
        u_re, u_im = scale / MODES * jnp.cos(angle), -scale / MODES * jnp.sin(angle)
        t_re, t_im = even[jnp.abs(apart)], direction * odd[jnp.abs(apart)]
        h_re, h_im = even[together], odd[together]
        a_re, a_im = t_re * u_re + t_im * u_im, t_im * u_re - t_re * u_im
        b_re, b_im = h_re * u_re - h_im * u_im, h_im * u_re + h_re * u_im
        c_re, c_im = u_re[:, None], u_im[:, None]
        p_re, p_im, m_re, m_im = a_re + b_re, a_im + b_im, a_re - b_re, a_im - b_im
        upper = jnp.concatenate([c_re * p_re - c_im * p_im, -(c_re * m_im + c_im * m_re)], axis=1)
        lower = jnp.concatenate([c_re * p_im + c_im * p_re, c_re * m_re - c_im * m_im], axis=1)
        factor = MODES / (OBS_VAR * math.sqrt(MODES))
        o_re, o_im = rows[6] * factor, rows[7] * factor
        info = jnp.concatenate([o_re * u_re - o_im * u_im, o_re * u_im + o_im * u_re])
        return jnp.concatenate([upper, lower], axis=0), info

    def passed(index, state):
        lost, message = state
        precision, info = node(index)
        excess = precision + lost
        inverse = newton_inverse(jnp.diag(1.0 / twice) + excess)
        lost = twice[:, None] * exact_dot(excess, inverse)
        return 0.5 * (lost + lost.T), exact_dot(inverse, info + message)

    start = (jnp.zeros((WIDTH, WIDTH), jnp.float32), jnp.zeros((WIDTH,), jnp.float32))
    before = lax.fori_loop(0, time, passed, start)
    after = lax.fori_loop(
        0, steps - 1 - time, lambda index, state: passed(steps - 1 - index, state), start
    )
    precision, info = node(time)
    base = jnp.diag((1.0 - twice * twice) / twice)
    inverse = newton_inverse(base + precision + before[0] + after[0])
    angle = time.astype(jnp.float32) * frequencies
    cosine, sine = jnp.diag(scale * jnp.cos(angle)), jnp.diag(scale * jnp.sin(angle))
    back = jnp.stack(
        [jnp.concatenate([cosine, -sine], axis=1), jnp.concatenate([sine, cosine], axis=1)], axis=1
    ).reshape(WIDTH, WIDTH)
    mine = exact_dot(lax.dynamic_slice_in_dim(back, shard * block, block, 0), inverse)
    mean = exact_dot(mine, info + before[1] + after[1])
    return mean[None], exact_dot(mine, back, NT)


def statistics(site_row, obs_row, count):
    transform, twiddles = tables()
    vmem = pl.BlockSpec(memory_space=pltpu.VMEM)
    return pl.pallas_call(
        statistics_kernel,
        out_shape=jax.ShapeDtypeStruct((8, MODES), jnp.float32),
        in_specs=[pl.BlockSpec(memory_space=pltpu.SMEM)] + [vmem] * 4,
        out_specs=vmem,
        name="statistics",
    )(count, site_row, obs_row, jnp.asarray(transform), jnp.asarray(twiddles))


def local(observations, site_ids, counts, frequencies, decay, proc_var):
    steps = lax.axis_size("tm")
    block = WIDTH // lax.axis_size("rows")
    stats = statistics(site_ids, observations, counts)
    copies = jnp.broadcast_to(stats, (steps, *stats.shape))
    everyone = lax.all_to_all(copies, "tm", split_axis=0, concat_axis=0, tiled=True)
    place = jnp.stack([lax.axis_index("tm"), lax.axis_index("rows")]).astype(jnp.int32)
    mean, cov, check = solve(place, everyone, frequencies, decay, proc_var, block)
    measure = jnp.sum(check, axis=1)
    mean, cov = lax.cond(
        (measure[0] <= CHAIN_LIMIT) & (measure[1] <= FINAL_LIMIT),
        lambda place, everyone, mean, cov: (mean, cov),
        lambda place, everyone, mean, cov: general(
            place, everyone, frequencies, decay, proc_var, block
        ),
        place,
        everyone,
        mean,
        cov,
    )
    return mean, cov[None]


def solution(mesh):
    return jax.shard_map(
        local,
        mesh=mesh,
        in_specs=(P("tm", None), P("tm", None), P("tm"), P(), P(), P()),
        out_specs=(P("tm", "rows"), P("tm", "rows", None)),
        check_vma=False,
    )
```

```python
import math

import jax
import jax.numpy as jnp
import numpy as np
from jax import lax
from jax.experimental import pallas as pl
from jax.experimental.pallas import tpu as pltpu
from jax.sharding import PartitionSpec as P

GRID = 4096
OBS_VAR = 64
MODES = 128
WIDTH = 2 * MODES
LOW = 32
HIGH = GRID // LOW
CHAIN_LIMIT = 1e-4
FINAL_LIMIT = 1e-2
NEWTON_STEPS = 30

NN = (((1,), (0,)), ((), ()))
NT = (((1,), (1,)), ((), ()))


def tables():
    order = np.arange(MODES, dtype=np.int64)
    high = np.arange(HIGH, dtype=np.int64)
    low = np.arange(LOW, dtype=np.int64)
    turn = 2.0 * math.pi * ((high[:, None] * order[None, :]) % HIGH) / HIGH
    transform = np.concatenate([np.cos(turn), np.sin(turn)], axis=1)
    far_back = 2 * MODES + 1 - order
    far_back[0] = MODES + 1
    twiddles = []
    for multiples in (order, far_back, MODES - order, order + 1):
        turn = 2.0 * math.pi * ((low[:, None] * multiples[None, :]) % GRID) / GRID
        twiddles += [np.cos(turn), np.sin(turn)]
    return transform.astype(np.float32), np.stack(twiddles).astype(np.float32)


def dot(left, right, dims=NN):
    return lax.dot_general(left, right, dims, preferred_element_type=jnp.float32)


def exact_dot(left, right, dims=None):
    dims = dims or (((1,), (0,)), ((), ()))
    return lax.dot_general(
        left, right, dims, precision=lax.Precision.HIGHEST, preferred_element_type=jnp.float32
    )


def rounded(array):
    return array.astype(jnp.bfloat16)


def split(array):
    upper = rounded(array)
    return upper, rounded(array - upper.astype(jnp.float32))


def dot3(left, right, dims=NN):
    a_hi, a_lo = left
    b_hi, b_lo = right
    (left_dim,), (right_dim,) = dims[0]
    return dot(
        jnp.concatenate([a_hi, a_hi, a_lo], axis=left_dim),
        jnp.concatenate([b_hi, b_lo, b_hi], axis=right_dim),
        dims,
    )


def iota(shape, dim):
    return lax.broadcasted_iota(jnp.int32, shape, dim)


def statistics_kernel(count_ref, site_ref, obs_ref, transform_ref, twiddle_ref, out_ref):
    sites = site_ref.shape[1]
    site = site_ref[...]
    live = iota((1, sites), 1) < count_ref[0]
    low = jnp.where(live, site & (LOW - 1), LOW)
    high = site >> (LOW.bit_length() - 1)
    obs = obs_ref[...]
    first = rounded(obs).astype(jnp.float32)
    second = rounded(obs - first).astype(jnp.float32)
    third = obs - first - second
    here = iota((LOW, sites), 0) == low
    zero = jnp.zeros((LOW, sites), jnp.float32)
    stack = jnp.concatenate(
        [
            jnp.where(here, 1.0, zero),
            jnp.where(here, first, zero),
            jnp.where(here, second, zero),
            jnp.where(here, third, zero),
        ],
        axis=0,
    )
    columns = jnp.where(iota((HIGH, sites), 0) == high, 1.0, 0.0)
    binned = dot(rounded(stack), rounded(columns), NT)
    observed = binned[LOW : 2 * LOW] + binned[2 * LOW : 3 * LOW] + binned[3 * LOW :]
    waves = exact_dot(jnp.concatenate([binned[:LOW], observed], axis=0), transform_ref[...])
    real, imag = waves[:LOW, :MODES], waves[:LOW, MODES:]
    real_obs = pltpu.roll(waves[LOW:, :MODES], MODES - 1, 1)
    imag_obs = pltpu.roll(waves[LOW:, MODES:], MODES - 1, 1)
    turned = (pltpu.roll(real, 1, 1), pltpu.roll(-imag, 1, 1))
    sources = ((real, imag), turned, (real, -imag), (real_obs, imag_obs))
    rows = []
    for kind, (re, im) in enumerate(sources):
        cosine, sine = twiddle_ref[2 * kind], twiddle_ref[2 * kind + 1]
        rows.append(jnp.sum(re * cosine - im * sine, 0, keepdims=True))
        rows.append(jnp.sum(re * sine + im * cosine, 0, keepdims=True))
    tile = jnp.concatenate(rows, axis=0)
    for copy in range(out_ref.shape[0]):
        out_ref[copy] = tile


def toeplitz(ahead, behind):
    shape = (MODES, MODES)
    upper = pltpu.roll(jnp.broadcast_to(ahead, shape), 0, 1, stride=1, stride_axis=0)
    lower = pltpu.roll(jnp.broadcast_to(behind, shape), 0, 1, stride=1, stride_axis=0)
    return jnp.where(iota(shape, 1) >= iota(shape, 0), upper, lower)


def build_block(stats, phase, block_ref):
    u_re, u_im = phase[0:1], phase[1:2]
    columns = phase.T
    cr, ci = columns[:, 0:1], columns[:, 1:2]
    tr = toeplitz(stats[0:1], stats[4:5])
    ti = toeplitz(-stats[1:2], stats[5:6])
    start = iota((1, MODES), 1) == 0
    near = [
        jnp.where(start, stats[2 + i : 3 + i], pltpu.roll(stats[4 + i : 5 + i], 1, 1))
        for i in range(2)
    ]
    mirrored = jnp.concatenate(
        [toeplitz(near[0], stats[2:3]), toeplitz(near[1], stats[3:4])], axis=0
    )
    shape = (2 * MODES, MODES)
    row = iota(shape, 0) & (MODES - 1)
    mirror = rounded(jnp.where(row + iota(shape, 1) == MODES - 1, 1.0, 0.0))
    sums = dot(jnp.concatenate(split(mirrored), axis=1), mirror)
    hr, hi = sums[:MODES], sums[MODES:]
    a_re, a_im = tr * u_re + ti * u_im, ti * u_re - tr * u_im
    b_re, b_im = hr * u_re - hi * u_im, hi * u_re + hr * u_im
    p_re, p_im, m_re, m_im = a_re + b_re, a_im + b_im, a_re - b_re, a_im - b_im
    block_ref[:MODES, :MODES] = cr * p_re - ci * p_im
    block_ref[:MODES, MODES:] = -(cr * m_im + ci * m_re)
    block_ref[MODES:, :MODES] = cr * p_im + ci * p_re
    block_ref[MODES:, MODES:] = cr * m_re - ci * m_im
    scale = MODES / (OBS_VAR * math.sqrt(MODES))
    o_re, o_im = stats[6:7] * scale, stats[7:8] * scale
    return jnp.concatenate([o_re * u_re - o_im * u_im, o_re * u_im + o_im * u_re], axis=1)


def diagonal_mask():
    shape = (MODES, MODES)
    return jnp.where(iota(shape, 0) == iota(shape, 1), 1.0, 0.0)


def spread(row, mask):
    zero = jnp.zeros((MODES, MODES), jnp.float32)
    upper = jnp.concatenate([mask * row[:, :MODES], zero], axis=1)
    return jnp.concatenate([upper, jnp.concatenate([zero, mask * row[:, MODES:]], axis=1)], axis=0)


def diagonal_of(matrix, mask, axis):
    upper = jnp.sum(matrix[:MODES, :MODES] * mask, axis=axis, keepdims=True)
    lower = jnp.sum(matrix[MODES:, MODES:] * mask, axis=axis, keepdims=True)
    return jnp.concatenate([upper, lower], axis=1 - axis)


def off_diagonal(matrix, mask):
    other = 1.0 - mask
    upper = jnp.concatenate([matrix[:MODES, :MODES] * other, matrix[:MODES, MODES:]], axis=1)
    lower = jnp.concatenate([matrix[MODES:, :MODES], matrix[MODES:, MODES:] * other], axis=1)
    return jnp.concatenate([upper, lower], axis=0)


def jacobi(excess, base, mask):
    by_row = lax.rsqrt(base[1] + diagonal_of(excess, mask, 1))
    own = diagonal_of(excess, mask, 0)
    by_lane = lax.rsqrt(base[0] + own)
    scale = by_row * by_lane
    return -off_diagonal(excess, mask) * scale, scale, by_lane, own


def squares(array):
    return jnp.sum(array * array, axis=0, keepdims=True)


def chain_inverse(excess, base, damping, mask):
    residue, scale, by_lane, own = jacobi(excess, base, mask)
    parts = split(residue)
    second = dot3(parts, parts)
    first_two = residue + second
    rest = (first_two + dot(rounded(second), rounded(first_two))) * scale
    diagonal = by_lane * by_lane
    lost = spread(damping[0] * own * diagonal, mask) - rest
    return rest, diagonal, lost, squares(second)


def final_inverse(excess, base, damping, mask):
    residue, scale, by_lane, _ = jacobi(excess, base, mask)
    parts = split(residue)
    second = dot3(parts, parts)
    second_hi = rounded(second)
    near = residue + second + dot(parts[0], second_hi)
    fourth = dot(second_hi, second_hi)
    rest = near + fourth + dot(rounded(near), rounded(fourth))
    return rest * scale, by_lane * by_lane, None, squares(second)


def final_rows(excess, base, rows, mask):
    residue, _, by_lane, _ = jacobi(excess, base, mask)
    parts = split(residue)
    second = dot3(parts, parts)
    second_parts = split(second)
    fourth = rounded(dot(second_parts[0], second_parts[0]))
    value = rows * by_lane
    value = value + dot3(split(value), parts)
    value = value + dot3(split(value), second_parts)
    value = value + dot(rounded(value), fourth)
    return value * by_lane, squares(second)


def product3(left, right, dims=NN):
    return dot3(split(left), split(right), dims)


def eliminate(carried, kept, rest, diagonal, mask, product):
    moved = carried * diagonal + product(carried, rest)
    return moved, moved * kept + product(moved, carried[:WIDTH] - spread(kept, mask), NT)


def solve_kernel(
    place_ref,
    stats_ref,
    frequency_ref,
    decay_ref,
    variance_ref,
    mean_ref,
    cov_ref,
    check_ref,
    phase_ref,
    block1_ref,
    block2_ref,
    rest1_ref,
    rest2_ref,
    lost1_ref,
    lost2_ref,
    saved_ref,
    far_ref,
    carried_ref,
    rows_ref,
    columns_ref,
):
    steps = stats_ref.shape[0]
    half = steps // 2
    time, shard = place_ref[0], place_ref[1]
    flip = time < half
    node = jnp.where(flip, steps - 1 - time, time)
    outer = steps - 1 - node

    def time_of(index):
        return jnp.where(flip, steps - 1 - index, index)

    decays = jnp.exp(-decay_ref[...])
    scale = jnp.sqrt(variance_ref[...] / decays)
    positions = iota((steps, MODES), 0)
    angles = time_of(positions).astype(jnp.float32) * frequency_ref[...]
    cosines = jnp.cos(angles) * (scale / MODES)
    sines = jnp.sin(angles) * (-scale / MODES)
    for index in range(steps):
        phase_ref[index, 0:1, :] = cosines[index : index + 1]
        phase_ref[index, 1:2, :] = sines[index : index + 1]
        phase_ref[index, 2:8, :] = jnp.zeros((6, MODES), jnp.float32)
    twice = jnp.concatenate([decays, decays], axis=1)
    own_base = (1.0 - twice * twice) / twice
    values = (twice, 1.0 / twice, own_base)
    table = jnp.concatenate(values + (jnp.zeros((5, WIDTH), jnp.float32),), axis=0)
    columns_ref[:MODES] = table[:, :MODES].T
    columns_ref[MODES:] = table[:, MODES:].T
    damping, base, own_base = (
        (value, columns_ref[:, i : i + 1]) for i, value in enumerate(values)
    )

    def build(index, block_ref):
        return build_block(stats_ref[time_of(index)], phase_ref[index], block_ref)

    def second_node(index):
        late = jnp.where(index >= half - 1, node, half + index - outer)
        return jnp.where(index < outer, steps - 1 - index, late)

    def run(invert_chain, invert_middle, finish, product):
        mask = diagonal_mask()
        ones = jnp.ones((1, WIDTH), jnp.float32)
        for ref in (rest1_ref, rest2_ref, lost1_ref, lost2_ref, saved_ref, far_ref, carried_ref):
            ref[...] = jnp.zeros(ref.shape, jnp.float32)
        rows_ref[...] = jnp.zeros(rows_ref.shape, jnp.float32)
        check_ref[...] = jnp.zeros(check_ref.shape, jnp.float32)
        rows_ref[8:9, :] = build(0, block1_ref)
        rows_ref[16:17, :] = build(second_node(0), block2_ref)

        def advance(index):
            @pl.when(index == outer)
            def _():
                message = carried_ref[WIDTH:]
                saved_ref[...] = lost2_ref[...]
                rows_ref[24:32, :] = message * rows_ref[33:34, :] + product(message, rest2_ref[...])
                eye = spread(ones, mask)
                lost2_ref[...] = spread(damping[0], mask)
                rest2_ref[...] = jnp.zeros((WIDTH, WIDTH), jnp.float32)
                rows_ref[33:35, :] = jnp.ones((2, WIDTH), jnp.float32)
                carried_ref[:WIDTH] = eye
                carried_ref[WIDTH:] = jnp.zeros((8, WIDTH), jnp.float32)
                far_ref[:WIDTH] = -eye
                far_ref[WIDTH:] = jnp.zeros((8, WIDTH), jnp.float32)

            excess1 = block1_ref[...] + lost1_ref[...]
            excess2 = block2_ref[...] + lost2_ref[...]
            diagonal1, diagonal2 = rows_ref[32:33, :], rows_ref[33:34, :]
            before = rows_ref[0:8, :]
            info1 = rows_ref[8:16, :] + before * diagonal1 + product(before, rest1_ref[...])
            kept = rows_ref[34:35, :]
            moved, left = eliminate(
                carried_ref[...], kept, rest2_ref[...], diagonal2, mask, product
            )
            rows_ref[34:35, :] = kept * diagonal2
            far_ref[...] += left
            carried_ref[:WIDTH] = moved[:WIDTH]
            info2 = moved[WIDTH:] + rows_ref[16:24, :]
            carried_ref[WIDTH:] = info2
            rows_ref[0:8, :] = info1
            return excess1, excess2, info1, info2

        def body(index, _):
            excess1, excess2, _, _ = advance(index)
            next1 = invert_chain(excess1, base, damping, mask)
            next2 = invert_chain(excess2, base, damping, mask)
            rest1_ref[...], rows_ref[32:33, :], lost1_ref[...] = next1
            rest2_ref[...], rows_ref[33:34, :], lost2_ref[...] = next2
            rows_ref[8:9, :] = build(index + 1, block1_ref)
            rows_ref[16:17, :] = build(second_node(index + 1), block2_ref)
            return 0

        lax.fori_loop(0, half - 1, body, 0)
        excess1, excess2, info1, info2 = advance(half - 1)
        rest, diagonal, _ = invert_middle(excess1 - far_ref[:WIDTH], base, damping, mask)
        carried_ref[:WIDTH] = carried_ref[:WIDTH].T
        carried_ref[WIDTH:] = info1 + far_ref[WIDTH:]
        _, left = eliminate(carried_ref[...], rows_ref[34:35, :], rest, diagonal, mask, product)
        excess = excess2 + saved_ref[...] - left[:WIDTH]
        info = info2 + rows_ref[24:32, :] + left[WIDTH:]

        block = cov_ref.shape[0]
        cosine = phase_ref[node, 0:1, :] * MODES
        sine = phase_ref[node, 1:2, :] * (-MODES)
        even = jnp.concatenate([cosine, -sine], axis=1)
        odd = jnp.concatenate([sine, cosine], axis=1)

        def turn_back(rows, start):
            row = iota((rows, WIDTH), 0) + start
            lane = iota((rows, WIDTH), 1) & (MODES - 1)
            value = jnp.where((row & 1) == 0, even, odd)
            return jnp.where(lane == (row >> 1), value, 0.0)

        mine = turn_back(block, shard * block)
        whole = split(turn_back(WIDTH, 0))
        (result,) = finish(excess, own_base, jnp.concatenate([mine, info], axis=0), mask)
        mean_ref[...] = dot3(split(result[block:]), split(mine), NT)[0:1]
        cov_ref[...] = dot3(split(result[:block]), whole, NT)

    def noted(inverse, row):
        def call(*args):
            *value, measure = inverse(*args)
            check_ref[row : row + 1, :] = jnp.maximum(check_ref[row : row + 1, :], measure)
            return value

        return call

    run(noted(chain_inverse, 0), noted(final_inverse, 1), noted(final_rows, 1), product3)


def solve(place, stats, frequencies, decay, proc_var, block):
    square = pltpu.VMEM((WIDTH, WIDTH), jnp.float32)
    tall = pltpu.VMEM((WIDTH + 8, WIDTH), jnp.float32)
    vmem = pl.BlockSpec(memory_space=pltpu.VMEM)
    return pl.pallas_call(
        solve_kernel,
        out_shape=(
            jax.ShapeDtypeStruct((1, block), jnp.float32),
            jax.ShapeDtypeStruct((block, WIDTH), jnp.float32),
            jax.ShapeDtypeStruct((2, WIDTH), jnp.float32),
        ),
        in_specs=[pl.BlockSpec(memory_space=pltpu.SMEM)] + [vmem] * 4,
        out_specs=(vmem, vmem, vmem),
        scratch_shapes=[
            pltpu.VMEM((stats.shape[0], 8, MODES), jnp.float32),
            *[square] * 7,
            tall,
            tall,
            pltpu.VMEM((40, WIDTH), jnp.float32),
            pltpu.VMEM((WIDTH, 8), jnp.float32),
        ],
        compiler_params=pltpu.CompilerParams(vmem_limit_bytes=48 << 20),
        name="solve",
    )(place, stats, frequencies[None], decay[None], proc_var[None])


def newton_inverse(matrix):
    eye = jnp.eye(WIDTH, dtype=jnp.float32)
    start = eye / jnp.sum(jnp.abs(matrix), axis=1, keepdims=True)

    def step(_, approx):
        return approx + exact_dot(approx, eye - exact_dot(matrix, approx))

    return lax.fori_loop(0, NEWTON_STEPS, step, start)


def general(place, stats, frequencies, decay, proc_var, block):
    steps = stats.shape[0]
    time, shard = place[0], place[1]
    damping = jnp.exp(-decay)
    scale = jnp.sqrt(proc_var / damping)
    twice = jnp.concatenate([damping, damping])
    order = jnp.arange(1, MODES + 1)
    apart, together = order[:, None] - order[None, :], order[:, None] + order[None, :]
    direction = jnp.sign(apart).astype(jnp.float32)

    def node(index):
        rows = stats[index]
        even = jnp.concatenate([rows[0], rows[4, :1], rows[2, :1], rows[2, :0:-1]])
        odd = jnp.concatenate([rows[1], rows[5, :1], rows[3, :1], rows[3, :0:-1]])
        angle = index.astype(jnp.float32) * frequencies
        u_re, u_im = scale / MODES * jnp.cos(angle), -scale / MODES * jnp.sin(angle)
        t_re, t_im = even[jnp.abs(apart)], direction * odd[jnp.abs(apart)]
        h_re, h_im = even[together], odd[together]
        a_re, a_im = t_re * u_re + t_im * u_im, t_im * u_re - t_re * u_im
        b_re, b_im = h_re * u_re - h_im * u_im, h_im * u_re + h_re * u_im
        c_re, c_im = u_re[:, None], u_im[:, None]
        p_re, p_im, m_re, m_im = a_re + b_re, a_im + b_im, a_re - b_re, a_im - b_im
        upper = jnp.concatenate([c_re * p_re - c_im * p_im, -(c_re * m_im + c_im * m_re)], axis=1)
        lower = jnp.concatenate([c_re * p_im + c_im * p_re, c_re * m_re - c_im * m_im], axis=1)
        factor = MODES / (OBS_VAR * math.sqrt(MODES))
        o_re, o_im = rows[6] * factor, rows[7] * factor
        info = jnp.concatenate([o_re * u_re - o_im * u_im, o_re * u_im + o_im * u_re])
        return jnp.concatenate([upper, lower], axis=0), info

    def passed(index, state):
        lost, message = state
        precision, info = node(index)
        excess = precision + lost
        inverse = newton_inverse(jnp.diag(1.0 / twice) + excess)
        lost = twice[:, None] * exact_dot(excess, inverse)
        return 0.5 * (lost + lost.T), exact_dot(inverse, info + message)

    start = (jnp.zeros((WIDTH, WIDTH), jnp.float32), jnp.zeros((WIDTH,), jnp.float32))
    before = lax.fori_loop(0, time, passed, start)
    after = lax.fori_loop(
        0, steps - 1 - time, lambda index, state: passed(steps - 1 - index, state), start
    )
    precision, info = node(time)
    base = jnp.diag((1.0 - twice * twice) / twice)
    inverse = newton_inverse(base + precision + before[0] + after[0])
    angle = time.astype(jnp.float32) * frequencies
    cosine, sine = jnp.diag(scale * jnp.cos(angle)), jnp.diag(scale * jnp.sin(angle))
    back = jnp.stack(
        [jnp.concatenate([cosine, -sine], axis=1), jnp.concatenate([sine, cosine], axis=1)], axis=1
    ).reshape(WIDTH, WIDTH)
    mine = exact_dot(lax.dynamic_slice_in_dim(back, shard * block, block, 0), inverse)
    mean = exact_dot(mine, info + before[1] + after[1])
    return mean[None], exact_dot(mine, back, NT)


def statistics(site_row, obs_row, count, copies):
    transform, twiddles = tables()
    vmem = pl.BlockSpec(memory_space=pltpu.VMEM)
    return pl.pallas_call(
        statistics_kernel,
        out_shape=jax.ShapeDtypeStruct((copies, 8, MODES), jnp.float32),
        in_specs=[pl.BlockSpec(memory_space=pltpu.SMEM)] + [vmem] * 4,
        out_specs=vmem,
        name="statistics",
    )(count, site_row, obs_row, jnp.asarray(transform), jnp.asarray(twiddles))


def local(observations, site_ids, counts, frequencies, decay, proc_var):
    steps = lax.axis_size("tm")
    block = WIDTH // lax.axis_size("rows")
    copies = statistics(site_ids, observations, counts, steps)
    everyone = lax.all_to_all(copies, "tm", split_axis=0, concat_axis=0, tiled=True)
    place = jnp.stack([lax.axis_index("tm"), lax.axis_index("rows")]).astype(jnp.int32)
    mean, cov, check = solve(place, everyone, frequencies, decay, proc_var, block)
    measure = jnp.sum(check, axis=1)
    mean, cov = lax.cond(
        (measure[0] <= CHAIN_LIMIT) & (measure[1] <= FINAL_LIMIT),
        lambda place, everyone, mean, cov: (mean, cov),
        lambda place, everyone, mean, cov: general(
            place, everyone, frequencies, decay, proc_var, block
        ),
        place,
        everyone,
        mean,
        cov,
    )
    return mean, cov[None]


def solution(mesh):
    return jax.shard_map(
        local,
        mesh=mesh,
        in_specs=(P("tm", None), P("tm", None), P("tm"), P(), P(), P()),
        out_specs=(P("tm", "rows"), P("tm", "rows", None)),
        check_vma=False,
    )
```

```python
import math

import jax
import jax.numpy as jnp
import numpy as np
from jax import lax
from jax.experimental import pallas as pl
from jax.experimental.pallas import tpu as pltpu
from jax.sharding import PartitionSpec as P

GRID = 4096
OBS_VAR = 64
MODES = 128
WIDTH = 2 * MODES
LOW = 32
HIGH = GRID // LOW
CHAIN_LIMIT = 1e-4
FINAL_LIMIT = 1e-2
NEWTON_STEPS = 30

NN = (((1,), (0,)), ((), ()))
NT = (((1,), (1,)), ((), ()))


def tables():
    order = np.arange(MODES, dtype=np.int64)
    high = np.arange(HIGH, dtype=np.int64)
    low = np.arange(LOW, dtype=np.int64)
    turn = 2.0 * math.pi * ((high[:, None] * order[None, :]) % HIGH) / HIGH
    transform = np.concatenate([np.cos(turn), np.sin(turn)], axis=1)
    far_back = 2 * MODES + 1 - order
    far_back[0] = MODES + 1
    twiddles = []
    for multiples in (order, far_back, MODES - order, order + 1):
        turn = 2.0 * math.pi * ((low[:, None] * multiples[None, :]) % GRID) / GRID
        twiddles += [np.cos(turn), np.sin(turn)]
    return transform.astype(np.float32), np.stack(twiddles).astype(np.float32)


def dot(left, right, dims=NN):
    return lax.dot_general(left, right, dims, preferred_element_type=jnp.float32)


def exact_dot(left, right, dims=None):
    dims = dims or (((1,), (0,)), ((), ()))
    return lax.dot_general(
        left, right, dims, precision=lax.Precision.HIGHEST, preferred_element_type=jnp.float32
    )


def rounded(array):
    return array.astype(jnp.bfloat16)


def split(array):
    upper = rounded(array)
    return upper, rounded(array - upper.astype(jnp.float32))


def dot3(left, right, dims=NN):
    a_hi, a_lo = left
    b_hi, b_lo = right
    (left_dim,), (right_dim,) = dims[0]
    return dot(
        jnp.concatenate([a_hi, a_hi, a_lo], axis=left_dim),
        jnp.concatenate([b_hi, b_lo, b_hi], axis=right_dim),
        dims,
    )


def iota(shape, dim):
    return lax.broadcasted_iota(jnp.int32, shape, dim)


def statistics_kernel(count_ref, site_ref, obs_ref, transform_ref, twiddle_ref, out_ref):
    sites = site_ref.shape[1]
    site = site_ref[...]
    live = iota((1, sites), 1) < count_ref[0]
    low = jnp.where(live, site & (LOW - 1), LOW)
    high = site >> (LOW.bit_length() - 1)
    obs = obs_ref[...]
    first = rounded(obs).astype(jnp.float32)
    second = rounded(obs - first).astype(jnp.float32)
    third = obs - first - second
    here = iota((LOW, sites), 0) == low
    zero = jnp.zeros((LOW, sites), jnp.float32)
    stack = jnp.concatenate(
        [
            jnp.where(here, 1.0, zero),
            jnp.where(here, first, zero),
            jnp.where(here, second, zero),
            jnp.where(here, third, zero),
        ],
        axis=0,
    )
    columns = jnp.where(iota((HIGH, sites), 0) == high, 1.0, 0.0)
    binned = dot(rounded(stack), rounded(columns), NT)
    observed = binned[LOW : 2 * LOW] + binned[2 * LOW : 3 * LOW] + binned[3 * LOW :]
    waves = exact_dot(jnp.concatenate([binned[:LOW], observed], axis=0), transform_ref[...])
    real, imag = waves[:LOW, :MODES], waves[:LOW, MODES:]
    real_obs = pltpu.roll(waves[LOW:, :MODES], MODES - 1, 1)
    imag_obs = pltpu.roll(waves[LOW:, MODES:], MODES - 1, 1)
    turned = (pltpu.roll(real, 1, 1), pltpu.roll(-imag, 1, 1))
    sources = ((real, imag), turned, (real, -imag), (real_obs, imag_obs))
    rows = []
    for kind, (re, im) in enumerate(sources):
        cosine, sine = twiddle_ref[2 * kind], twiddle_ref[2 * kind + 1]
        rows.append(jnp.sum(re * cosine - im * sine, 0, keepdims=True))
        rows.append(jnp.sum(re * sine + im * cosine, 0, keepdims=True))
    tile = jnp.concatenate(rows, axis=0)
    for copy in range(out_ref.shape[0]):
        out_ref[copy] = tile


def toeplitz(ahead, behind):
    shape = (MODES, MODES)
    upper = pltpu.roll(jnp.broadcast_to(ahead, shape), 0, 1, stride=1, stride_axis=0)
    lower = pltpu.roll(jnp.broadcast_to(behind, shape), 0, 1, stride=1, stride_axis=0)
    return jnp.where(iota(shape, 1) >= iota(shape, 0), upper, lower)


def build_block(stats, phase, block_ref):
    u_re, u_im = phase[0:1], phase[1:2]
    columns = phase.T
    cr, ci = columns[:, 0:1], columns[:, 1:2]
    tr = toeplitz(stats[0:1], stats[4:5])
    ti = toeplitz(-stats[1:2], stats[5:6])
    start = iota((1, MODES), 1) == 0
    near = [
        jnp.where(start, stats[2 + i : 3 + i], pltpu.roll(stats[4 + i : 5 + i], 1, 1))
        for i in range(2)
    ]
    mirrored = jnp.concatenate(
        [toeplitz(near[0], stats[2:3]), toeplitz(near[1], stats[3:4])], axis=0
    )
    shape = (2 * MODES, MODES)
    row = iota(shape, 0) & (MODES - 1)
    mirror = rounded(jnp.where(row + iota(shape, 1) == MODES - 1, 1.0, 0.0))
    sums = dot(jnp.concatenate(split(mirrored), axis=1), mirror)
    hr, hi = sums[:MODES], sums[MODES:]
    a_re, a_im = tr * u_re + ti * u_im, ti * u_re - tr * u_im
    b_re, b_im = hr * u_re - hi * u_im, hi * u_re + hr * u_im
    p_re, p_im, m_re, m_im = a_re + b_re, a_im + b_im, a_re - b_re, a_im - b_im
    block_ref[:MODES, :MODES] = cr * p_re - ci * p_im
    block_ref[:MODES, MODES:] = -(cr * m_im + ci * m_re)
    block_ref[MODES:, :MODES] = cr * p_im + ci * p_re
    block_ref[MODES:, MODES:] = cr * m_re - ci * m_im
    scale = MODES / (OBS_VAR * math.sqrt(MODES))
    o_re, o_im = stats[6:7] * scale, stats[7:8] * scale
    return jnp.concatenate([o_re * u_re - o_im * u_im, o_re * u_im + o_im * u_re], axis=1)


def diagonal_mask():
    shape = (MODES, MODES)
    return jnp.where(iota(shape, 0) == iota(shape, 1), 1.0, 0.0)


def spread(row, mask):
    zero = jnp.zeros((MODES, MODES), jnp.float32)
    upper = jnp.concatenate([mask * row[:, :MODES], zero], axis=1)
    return jnp.concatenate([upper, jnp.concatenate([zero, mask * row[:, MODES:]], axis=1)], axis=0)


def diagonal_of(matrix, mask, axis):
    upper = jnp.sum(matrix[:MODES, :MODES] * mask, axis=axis, keepdims=True)
    lower = jnp.sum(matrix[MODES:, MODES:] * mask, axis=axis, keepdims=True)
    return jnp.concatenate([upper, lower], axis=1 - axis)


def off_diagonal(matrix, mask):
    other = 1.0 - mask
    upper = jnp.concatenate([matrix[:MODES, :MODES] * other, matrix[:MODES, MODES:]], axis=1)
    lower = jnp.concatenate([matrix[MODES:, :MODES], matrix[MODES:, MODES:] * other], axis=1)
    return jnp.concatenate([upper, lower], axis=0)


def jacobi(excess, base, mask):
    by_row = lax.rsqrt(base[1] + diagonal_of(excess, mask, 1))
    own = diagonal_of(excess, mask, 0)
    by_lane = lax.rsqrt(base[0] + own)
    scale = by_row * by_lane
    return -off_diagonal(excess, mask) * scale, scale, by_lane, own


def squares(array):
    return jnp.sum(array * array, axis=0, keepdims=True)


def chain_inverse(excess, base, damping, mask):
    residue, scale, by_lane, own = jacobi(excess, base, mask)
    parts = split(residue)
    second = dot3(parts, parts)
    first_two = residue + second
    rest = (first_two + dot(rounded(second), rounded(first_two))) * scale
    diagonal = by_lane * by_lane
    lost = spread(damping[0] * own * diagonal, mask) - rest
    return rest, diagonal, lost, squares(second)


def final_inverse(excess, base, damping, mask):
    residue, scale, by_lane, _ = jacobi(excess, base, mask)
    parts = split(residue)
    second = dot3(parts, parts)
    second_hi = rounded(second)
    near = residue + second + dot(parts[0], second_hi)
    fourth = dot(second_hi, second_hi)
    rest = near + fourth + dot(rounded(near), rounded(fourth))
    return rest * scale, by_lane * by_lane, None, squares(second)


def final_rows(excess, base, rows, mask):
    residue, _, by_lane, _ = jacobi(excess, base, mask)
    parts = split(residue)
    second = dot3(parts, parts)
    second_parts = split(second)
    fourth = rounded(dot(second_parts[0], second_parts[0]))
    value = rows * by_lane
    value = value + dot3(split(value), parts)
    value = value + dot3(split(value), second_parts)
    value = value + dot(rounded(value), fourth)
    return value * by_lane, squares(second)


def product3(left, right, dims=NN):
    return dot3(split(left), split(right), dims)


def eliminate(carried, kept, rest, diagonal, mask, product):
    moved = carried * diagonal + product(carried, rest)
    return moved, moved * kept + product(moved, carried[:WIDTH] - spread(kept, mask), NT)


def solve_kernel(
    place_ref,
    stats_ref,
    frequency_ref,
    decay_ref,
    variance_ref,
    mean_ref,
    cov_ref,
    flag_ref,
    phase_ref,
    block1_ref,
    block2_ref,
    rest1_ref,
    rest2_ref,
    lost1_ref,
    lost2_ref,
    saved_ref,
    far_ref,
    carried_ref,
    rows_ref,
    columns_ref,
    check_ref,
):
    steps = stats_ref.shape[0]
    half = steps // 2
    time, shard = place_ref[0], place_ref[1]
    flip = time < half
    node = jnp.where(flip, steps - 1 - time, time)
    outer = steps - 1 - node

    def time_of(index):
        return jnp.where(flip, steps - 1 - index, index)

    decays = jnp.exp(-decay_ref[...])
    scale = jnp.sqrt(variance_ref[...] / decays)
    positions = iota((steps, MODES), 0)
    angles = time_of(positions).astype(jnp.float32) * frequency_ref[...]
    cosines = jnp.cos(angles) * (scale / MODES)
    sines = jnp.sin(angles) * (-scale / MODES)
    for index in range(steps):
        phase_ref[index, 0:1, :] = cosines[index : index + 1]
        phase_ref[index, 1:2, :] = sines[index : index + 1]
        phase_ref[index, 2:8, :] = jnp.zeros((6, MODES), jnp.float32)
    twice = jnp.concatenate([decays, decays], axis=1)
    own_base = (1.0 - twice * twice) / twice
    values = (twice, 1.0 / twice, own_base)
    table = jnp.concatenate(values + (jnp.zeros((5, WIDTH), jnp.float32),), axis=0)
    columns_ref[:MODES] = table[:, :MODES].T
    columns_ref[MODES:] = table[:, MODES:].T
    damping, base, own_base = (
        (value, columns_ref[:, i : i + 1]) for i, value in enumerate(values)
    )

    def build(index, block_ref):
        return build_block(stats_ref[time_of(index)], phase_ref[index], block_ref)

    def second_node(index):
        late = jnp.where(index >= half - 1, node, half + index - outer)
        return jnp.where(index < outer, steps - 1 - index, late)

    def run(invert_chain, invert_middle, finish, product):
        mask = diagonal_mask()
        ones = jnp.ones((1, WIDTH), jnp.float32)
        for ref in (rest1_ref, rest2_ref, lost1_ref, lost2_ref, saved_ref, far_ref, carried_ref):
            ref[...] = jnp.zeros(ref.shape, jnp.float32)
        rows_ref[...] = jnp.zeros(rows_ref.shape, jnp.float32)
        check_ref[...] = jnp.zeros(check_ref.shape, jnp.float32)
        rows_ref[8:9, :] = build(0, block1_ref)
        rows_ref[16:17, :] = build(second_node(0), block2_ref)

        def advance(index):
            @pl.when(index == outer)
            def _():
                message = carried_ref[WIDTH:]
                saved_ref[...] = lost2_ref[...]
                rows_ref[24:32, :] = message * rows_ref[33:34, :] + product(message, rest2_ref[...])
                eye = spread(ones, mask)
                lost2_ref[...] = spread(damping[0], mask)
                rest2_ref[...] = jnp.zeros((WIDTH, WIDTH), jnp.float32)
                rows_ref[33:35, :] = jnp.ones((2, WIDTH), jnp.float32)
                carried_ref[:WIDTH] = eye
                carried_ref[WIDTH:] = jnp.zeros((8, WIDTH), jnp.float32)
                far_ref[:WIDTH] = -eye
                far_ref[WIDTH:] = jnp.zeros((8, WIDTH), jnp.float32)

            excess1 = block1_ref[...] + lost1_ref[...]
            excess2 = block2_ref[...] + lost2_ref[...]
            diagonal1, diagonal2 = rows_ref[32:33, :], rows_ref[33:34, :]
            before = rows_ref[0:8, :]
            info1 = rows_ref[8:16, :] + before * diagonal1 + product(before, rest1_ref[...])
            kept = rows_ref[34:35, :]
            moved, left = eliminate(
                carried_ref[...], kept, rest2_ref[...], diagonal2, mask, product
            )
            rows_ref[34:35, :] = kept * diagonal2
            far_ref[...] += left
            carried_ref[:WIDTH] = moved[:WIDTH]
            info2 = moved[WIDTH:] + rows_ref[16:24, :]
            carried_ref[WIDTH:] = info2
            rows_ref[0:8, :] = info1
            return excess1, excess2, info1, info2

        def body(index, _):
            excess1, excess2, _, _ = advance(index)
            next1 = invert_chain(excess1, base, damping, mask)
            next2 = invert_chain(excess2, base, damping, mask)
            rest1_ref[...], rows_ref[32:33, :], lost1_ref[...] = next1
            rest2_ref[...], rows_ref[33:34, :], lost2_ref[...] = next2
            rows_ref[8:9, :] = build(index + 1, block1_ref)
            rows_ref[16:17, :] = build(second_node(index + 1), block2_ref)
            return 0

        lax.fori_loop(0, half - 1, body, 0)
        excess1, excess2, info1, info2 = advance(half - 1)
        rest, diagonal, _ = invert_middle(excess1 - far_ref[:WIDTH], base, damping, mask)
        carried_ref[:WIDTH] = carried_ref[:WIDTH].T
        carried_ref[WIDTH:] = info1 + far_ref[WIDTH:]
        _, left = eliminate(carried_ref[...], rows_ref[34:35, :], rest, diagonal, mask, product)
        excess = excess2 + saved_ref[...] - left[:WIDTH]
        info = info2 + rows_ref[24:32, :] + left[WIDTH:]

        block = cov_ref.shape[0]
        cosine = phase_ref[node, 0:1, :] * MODES
        sine = phase_ref[node, 1:2, :] * (-MODES)
        even = jnp.concatenate([cosine, -sine], axis=1)
        odd = jnp.concatenate([sine, cosine], axis=1)

        def turn_back(rows, start):
            row = iota((rows, WIDTH), 0) + start
            lane = iota((rows, WIDTH), 1) & (MODES - 1)
            value = jnp.where((row & 1) == 0, even, odd)
            return jnp.where(lane == (row >> 1), value, 0.0)

        mine = turn_back(block, shard * block)
        whole = split(turn_back(WIDTH, 0))
        (result,) = finish(excess, own_base, jnp.concatenate([mine, info], axis=0), mask)
        mean_ref[...] = dot3(split(result[block:]), split(mine), NT)[0:1]
        cov_ref[...] = dot3(split(result[:block]), whole, NT)

    def noted(inverse, row):
        def call(*args):
            *value, measure = inverse(*args)
            check_ref[row : row + 1, :] = jnp.maximum(check_ref[row : row + 1, :], measure)
            return value

        return call

    run(noted(chain_inverse, 0), noted(final_inverse, 1), noted(final_rows, 1), product3)
    chain, final = jnp.sum(check_ref[0:1, :]), jnp.sum(check_ref[1:2, :])
    flag_ref[0] = jnp.where((chain <= CHAIN_LIMIT) & (final <= FINAL_LIMIT), 1, 0)


def solve(place, stats, frequencies, decay, proc_var, block):
    square = pltpu.VMEM((WIDTH, WIDTH), jnp.float32)
    tall = pltpu.VMEM((WIDTH + 8, WIDTH), jnp.float32)
    vmem = pl.BlockSpec(memory_space=pltpu.VMEM)
    return pl.pallas_call(
        solve_kernel,
        out_shape=(
            jax.ShapeDtypeStruct((1, block), jnp.float32),
            jax.ShapeDtypeStruct((block, WIDTH), jnp.float32),
            jax.ShapeDtypeStruct((1,), jnp.int32),
        ),
        in_specs=[pl.BlockSpec(memory_space=pltpu.SMEM)] + [vmem] * 4,
        out_specs=(vmem, vmem, pl.BlockSpec(memory_space=pltpu.SMEM)),
        scratch_shapes=[
            pltpu.VMEM((stats.shape[0], 8, MODES), jnp.float32),
            *[square] * 7,
            tall,
            tall,
            pltpu.VMEM((40, WIDTH), jnp.float32),
            pltpu.VMEM((WIDTH, 8), jnp.float32),
            pltpu.VMEM((2, WIDTH), jnp.float32),
        ],
        compiler_params=pltpu.CompilerParams(vmem_limit_bytes=48 << 20),
        name="solve",
    )(place, stats, frequencies[None], decay[None], proc_var[None])


def newton_inverse(matrix):
    eye = jnp.eye(WIDTH, dtype=jnp.float32)
    start = eye / jnp.sum(jnp.abs(matrix), axis=1, keepdims=True)

    def step(_, approx):
        return approx + exact_dot(approx, eye - exact_dot(matrix, approx))

    return lax.fori_loop(0, NEWTON_STEPS, step, start)


def general(place, stats, frequencies, decay, proc_var, block):
    steps = stats.shape[0]
    time, shard = place[0], place[1]
    damping = jnp.exp(-decay)
    scale = jnp.sqrt(proc_var / damping)
    twice = jnp.concatenate([damping, damping])
    order = jnp.arange(1, MODES + 1)
    apart, together = order[:, None] - order[None, :], order[:, None] + order[None, :]
    direction = jnp.sign(apart).astype(jnp.float32)

    def node(index):
        rows = stats[index]
        even = jnp.concatenate([rows[0], rows[4, :1], rows[2, :1], rows[2, :0:-1]])
        odd = jnp.concatenate([rows[1], rows[5, :1], rows[3, :1], rows[3, :0:-1]])
        angle = index.astype(jnp.float32) * frequencies
        u_re, u_im = scale / MODES * jnp.cos(angle), -scale / MODES * jnp.sin(angle)
        t_re, t_im = even[jnp.abs(apart)], direction * odd[jnp.abs(apart)]
        h_re, h_im = even[together], odd[together]
        a_re, a_im = t_re * u_re + t_im * u_im, t_im * u_re - t_re * u_im
        b_re, b_im = h_re * u_re - h_im * u_im, h_im * u_re + h_re * u_im
        c_re, c_im = u_re[:, None], u_im[:, None]
        p_re, p_im, m_re, m_im = a_re + b_re, a_im + b_im, a_re - b_re, a_im - b_im
        upper = jnp.concatenate([c_re * p_re - c_im * p_im, -(c_re * m_im + c_im * m_re)], axis=1)
        lower = jnp.concatenate([c_re * p_im + c_im * p_re, c_re * m_re - c_im * m_im], axis=1)
        factor = MODES / (OBS_VAR * math.sqrt(MODES))
        o_re, o_im = rows[6] * factor, rows[7] * factor
        info = jnp.concatenate([o_re * u_re - o_im * u_im, o_re * u_im + o_im * u_re])
        return jnp.concatenate([upper, lower], axis=0), info

    def passed(index, state):
        lost, message = state
        precision, info = node(index)
        excess = precision + lost
        inverse = newton_inverse(jnp.diag(1.0 / twice) + excess)
        lost = twice[:, None] * exact_dot(excess, inverse)
        return 0.5 * (lost + lost.T), exact_dot(inverse, info + message)

    start = (jnp.zeros((WIDTH, WIDTH), jnp.float32), jnp.zeros((WIDTH,), jnp.float32))
    before = lax.fori_loop(0, time, passed, start)
    after = lax.fori_loop(
        0, steps - 1 - time, lambda index, state: passed(steps - 1 - index, state), start
    )
    precision, info = node(time)
    base = jnp.diag((1.0 - twice * twice) / twice)
    inverse = newton_inverse(base + precision + before[0] + after[0])
    angle = time.astype(jnp.float32) * frequencies
    cosine, sine = jnp.diag(scale * jnp.cos(angle)), jnp.diag(scale * jnp.sin(angle))
    back = jnp.stack(
        [jnp.concatenate([cosine, -sine], axis=1), jnp.concatenate([sine, cosine], axis=1)], axis=1
    ).reshape(WIDTH, WIDTH)
    mine = exact_dot(lax.dynamic_slice_in_dim(back, shard * block, block, 0), inverse)
    mean = exact_dot(mine, info + before[1] + after[1])
    return mean[None], exact_dot(mine, back, NT)


def statistics(site_row, obs_row, count, copies):
    transform, twiddles = tables()
    vmem = pl.BlockSpec(memory_space=pltpu.VMEM)
    return pl.pallas_call(
        statistics_kernel,
        out_shape=jax.ShapeDtypeStruct((copies, 8, MODES), jnp.float32),
        in_specs=[pl.BlockSpec(memory_space=pltpu.SMEM)] + [vmem] * 4,
        out_specs=vmem,
        name="statistics",
    )(count, site_row, obs_row, jnp.asarray(transform), jnp.asarray(twiddles))


def local(observations, site_ids, counts, frequencies, decay, proc_var):
    steps = lax.axis_size("tm")
    block = WIDTH // lax.axis_size("rows")
    copies = statistics(site_ids, observations, counts, steps)
    everyone = lax.all_to_all(copies, "tm", split_axis=0, concat_axis=0, tiled=True)
    place = jnp.stack([lax.axis_index("tm"), lax.axis_index("rows")]).astype(jnp.int32)
    mean, cov, flag = solve(place, everyone, frequencies, decay, proc_var, block)
    mean, cov = lax.cond(
        flag[0] == 1,
        lambda place, everyone, mean, cov: (mean, cov),
        lambda place, everyone, mean, cov: general(
            place, everyone, frequencies, decay, proc_var, block
        ),
        place,
        everyone,
        mean,
        cov,
    )
    return mean, cov[None]


def solution(mesh):
    return jax.shard_map(
        local,
        mesh=mesh,
        in_specs=(P("tm", None), P("tm", None), P("tm"), P(), P(), P()),
        out_specs=(P("tm", "rows"), P("tm", "rows", None)),
        check_vma=False,
    )
```

```python
import math

import jax
import jax.numpy as jnp
import numpy as np
from jax import lax
from jax.experimental import pallas as pl
from jax.experimental.pallas import tpu as pltpu
from jax.sharding import PartitionSpec as P

GRID = 4096
OBS_VAR = 64
MODES = 128
WIDTH = 2 * MODES
LOW = 32
HIGH = GRID // LOW
CHAIN_LIMIT = 1e-4
FINAL_LIMIT = 1e-2
NEWTON_STEPS = 30

NN = (((1,), (0,)), ((), ()))
NT = (((1,), (1,)), ((), ()))


def tables():
    order = np.arange(MODES, dtype=np.int64)
    high = np.arange(HIGH, dtype=np.int64)
    low = np.arange(LOW, dtype=np.int64)
    turn = 2.0 * math.pi * ((high[:, None] * order[None, :]) % HIGH) / HIGH
    transform = np.concatenate([np.cos(turn), np.sin(turn)], axis=1)
    far_back = 2 * MODES + 1 - order
    far_back[0] = MODES + 1
    twiddles = []
    for multiples in (order, far_back, MODES - order, order + 1):
        turn = 2.0 * math.pi * ((low[:, None] * multiples[None, :]) % GRID) / GRID
        twiddles += [np.cos(turn), np.sin(turn)]
    return transform.astype(np.float32), np.stack(twiddles).astype(np.float32)


def dot(left, right, dims=NN):
    return lax.dot_general(left, right, dims, preferred_element_type=jnp.float32)


def exact_dot(left, right, dims=None):
    dims = dims or (((1,), (0,)), ((), ()))
    return lax.dot_general(
        left, right, dims, precision=lax.Precision.HIGHEST, preferred_element_type=jnp.float32
    )


def rounded(array):
    return array.astype(jnp.bfloat16)


def split(array):
    upper = rounded(array)
    return upper, rounded(array - upper.astype(jnp.float32))


def dot3(left, right, dims=NN):
    a_hi, a_lo = left
    b_hi, b_lo = right
    (left_dim,), (right_dim,) = dims[0]
    return dot(
        jnp.concatenate([a_hi, a_hi, a_lo], axis=left_dim),
        jnp.concatenate([b_hi, b_lo, b_hi], axis=right_dim),
        dims,
    )


def iota(shape, dim):
    return lax.broadcasted_iota(jnp.int32, shape, dim)


def statistics_kernel(count_ref, site_ref, obs_ref, transform_ref, twiddle_ref, out_ref):
    sites = site_ref.shape[1]
    site = site_ref[...]
    live = iota((1, sites), 1) < count_ref[0]
    low = jnp.where(live, site & (LOW - 1), LOW)
    high = site >> (LOW.bit_length() - 1)
    obs = obs_ref[...]
    first = rounded(obs).astype(jnp.float32)
    second = rounded(obs - first).astype(jnp.float32)
    third = obs - first - second
    here = iota((LOW, sites), 0) == low
    zero = jnp.zeros((LOW, sites), jnp.float32)
    stack = jnp.concatenate(
        [
            jnp.where(here, 1.0, zero),
            jnp.where(here, first, zero),
            jnp.where(here, second, zero),
            jnp.where(here, third, zero),
        ],
        axis=0,
    )
    columns = jnp.where(iota((HIGH, sites), 0) == high, 1.0, 0.0)
    binned = dot(rounded(stack), rounded(columns), NT)
    observed = binned[LOW : 2 * LOW] + binned[2 * LOW : 3 * LOW] + binned[3 * LOW :]
    waves = exact_dot(jnp.concatenate([binned[:LOW], observed], axis=0), transform_ref[...])
    real, imag = waves[:LOW, :MODES], waves[:LOW, MODES:]
    real_obs = pltpu.roll(waves[LOW:, :MODES], MODES - 1, 1)
    imag_obs = pltpu.roll(waves[LOW:, MODES:], MODES - 1, 1)
    turned = (pltpu.roll(real, 1, 1), pltpu.roll(-imag, 1, 1))
    sources = ((real, imag), turned, (real, -imag), (real_obs, imag_obs))
    rows = []
    for kind, (re, im) in enumerate(sources):
        cosine, sine = twiddle_ref[2 * kind], twiddle_ref[2 * kind + 1]
        rows.append(jnp.sum(re * cosine - im * sine, 0, keepdims=True))
        rows.append(jnp.sum(re * sine + im * cosine, 0, keepdims=True))
    tile = jnp.concatenate(rows, axis=0)
    for copy in range(out_ref.shape[0]):
        out_ref[copy] = tile


def toeplitz(ahead, behind):
    shape = (MODES, MODES)
    upper = pltpu.roll(jnp.broadcast_to(ahead, shape), 0, 1, stride=1, stride_axis=0)
    lower = pltpu.roll(jnp.broadcast_to(behind, shape), 0, 1, stride=1, stride_axis=0)
    return jnp.where(iota(shape, 1) >= iota(shape, 0), upper, lower)


def build_block(stats, phase, block_ref):
    u_re, u_im = phase[0:1], phase[1:2]
    columns = phase.T
    cr, ci = columns[:, 0:1], columns[:, 1:2]
    tr = toeplitz(stats[0:1], stats[4:5])
    ti = toeplitz(-stats[1:2], stats[5:6])
    start = iota((1, MODES), 1) == 0
    near = [
        jnp.where(start, stats[2 + i : 3 + i], pltpu.roll(stats[4 + i : 5 + i], 1, 1))
        for i in range(2)
    ]
    mirrored = jnp.concatenate(
        [toeplitz(near[0], stats[2:3]), toeplitz(near[1], stats[3:4])], axis=0
    )
    shape = (2 * MODES, MODES)
    row = iota(shape, 0) & (MODES - 1)
    mirror = rounded(jnp.where(row + iota(shape, 1) == MODES - 1, 1.0, 0.0))
    sums = dot(jnp.concatenate(split(mirrored), axis=1), mirror)
    hr, hi = sums[:MODES], sums[MODES:]
    a_re, a_im = tr * u_re + ti * u_im, ti * u_re - tr * u_im
    b_re, b_im = hr * u_re - hi * u_im, hi * u_re + hr * u_im
    p_re, p_im, m_re, m_im = a_re + b_re, a_im + b_im, a_re - b_re, a_im - b_im
    block_ref[:MODES, :MODES] = cr * p_re - ci * p_im
    block_ref[:MODES, MODES:] = -(cr * m_im + ci * m_re)
    block_ref[MODES:, :MODES] = cr * p_im + ci * p_re
    block_ref[MODES:, MODES:] = cr * m_re - ci * m_im
    scale = MODES / (OBS_VAR * math.sqrt(MODES))
    o_re, o_im = stats[6:7] * scale, stats[7:8] * scale
    return jnp.concatenate([o_re * u_re - o_im * u_im, o_re * u_im + o_im * u_re], axis=1)


def diagonal_mask():
    shape = (MODES, MODES)
    return jnp.where(iota(shape, 0) == iota(shape, 1), 1.0, 0.0)


def spread(row, mask):
    zero = jnp.zeros((MODES, MODES), jnp.float32)
    upper = jnp.concatenate([mask * row[:, :MODES], zero], axis=1)
    return jnp.concatenate([upper, jnp.concatenate([zero, mask * row[:, MODES:]], axis=1)], axis=0)


def diagonal_of(matrix, mask, axis):
    upper = jnp.sum(matrix[:MODES, :MODES] * mask, axis=axis, keepdims=True)
    lower = jnp.sum(matrix[MODES:, MODES:] * mask, axis=axis, keepdims=True)
    return jnp.concatenate([upper, lower], axis=1 - axis)


def off_diagonal(matrix, mask):
    other = 1.0 - mask
    upper = jnp.concatenate([matrix[:MODES, :MODES] * other, matrix[:MODES, MODES:]], axis=1)
    lower = jnp.concatenate([matrix[MODES:, :MODES], matrix[MODES:, MODES:] * other], axis=1)
    return jnp.concatenate([upper, lower], axis=0)


def jacobi(excess, base, mask):
    by_row = lax.rsqrt(base[1] + diagonal_of(excess, mask, 1))
    own = diagonal_of(excess, mask, 0)
    by_lane = lax.rsqrt(base[0] + own)
    scale = by_row * by_lane
    return -off_diagonal(excess, mask) * scale, scale, by_lane, own


def squares(array):
    return jnp.sum(array * array, axis=0, keepdims=True)


def chain_inverse(excess, base, damping, mask):
    residue, scale, by_lane, own = jacobi(excess, base, mask)
    parts = split(residue)
    second = dot3(parts, parts)
    first_two = residue + second
    rest = (first_two + dot(rounded(second), rounded(first_two))) * scale
    diagonal = by_lane * by_lane
    lost = spread(damping[0] * own * diagonal, mask) - rest
    return rest, diagonal, lost, squares(second)


def final_inverse(excess, base, damping, mask):
    residue, scale, by_lane, _ = jacobi(excess, base, mask)
    parts = split(residue)
    second = dot3(parts, parts)
    second_hi = rounded(second)
    near = residue + second + dot(parts[0], second_hi)
    fourth = dot(second_hi, second_hi)
    rest = near + fourth + dot(rounded(near), rounded(fourth))
    return rest * scale, by_lane * by_lane, None, squares(second)


def final_rows(excess, base, rows, mask):
    residue, _, by_lane, _ = jacobi(excess, base, mask)
    parts = split(residue)
    second = dot3(parts, parts)
    second_parts = split(second)
    fourth = rounded(dot(second_parts[0], second_parts[0]))
    value = rows * by_lane
    value = value + dot3(split(value), parts)
    value = value + dot3(split(value), second_parts)
    value = value + dot(rounded(value), fourth)
    return value * by_lane, squares(second)


def product3(left, right, dims=NN):
    return dot3(split(left), split(right), dims)


def eliminate(carried, kept, rest, diagonal, mask, product):
    moved = carried * diagonal + product(carried, rest)
    return moved, moved * kept + product(moved, carried[:WIDTH] - spread(kept, mask), NT)


def solve_kernel(
    place_ref,
    stats_ref,
    frequency_ref,
    decay_ref,
    variance_ref,
    mean_ref,
    cov_ref,
    flag_ref,
    phase_ref,
    block1_ref,
    block2_ref,
    rest1_ref,
    rest2_ref,
    lost1_ref,
    lost2_ref,
    saved_ref,
    far_ref,
    carried_ref,
    rows_ref,
    columns_ref,
    check_ref,
):
    steps = stats_ref.shape[0]
    half = steps // 2
    time, shard = place_ref[0], place_ref[1]
    flip = time < half
    node = jnp.where(flip, steps - 1 - time, time)
    outer = steps - 1 - node

    def time_of(index):
        return jnp.where(flip, steps - 1 - index, index)

    decays = jnp.exp(-decay_ref[...])
    scale = jnp.sqrt(variance_ref[...] / decays)
    positions = iota((steps, MODES), 0)
    angles = time_of(positions).astype(jnp.float32) * frequency_ref[...]
    cosines = jnp.cos(angles) * (scale / MODES)
    sines = jnp.sin(angles) * (-scale / MODES)
    for index in range(steps):
        phase_ref[index, 0:1, :] = cosines[index : index + 1]
        phase_ref[index, 1:2, :] = sines[index : index + 1]
        phase_ref[index, 2:8, :] = jnp.zeros((6, MODES), jnp.float32)
    twice = jnp.concatenate([decays, decays], axis=1)
    own_base = (1.0 - twice * twice) / twice
    values = (twice, 1.0 / twice, own_base)
    table = jnp.concatenate(values + (jnp.zeros((5, WIDTH), jnp.float32),), axis=0)
    columns_ref[:MODES] = table[:, :MODES].T
    columns_ref[MODES:] = table[:, MODES:].T
    damping, base, own_base = (
        (value, columns_ref[:, i : i + 1]) for i, value in enumerate(values)
    )

    def build(index, block_ref):
        return build_block(stats_ref[time_of(index)], phase_ref[index], block_ref)

    def second_node(index):
        late = jnp.where(index >= half - 1, node, half + index - outer)
        return jnp.where(index < outer, steps - 1 - index, late)

    def run(invert_chain, invert_middle, finish, product):
        mask = diagonal_mask()
        ones = jnp.ones((1, WIDTH), jnp.float32)
        for ref in (rest1_ref, rest2_ref, lost1_ref, lost2_ref, saved_ref, far_ref, carried_ref):
            ref[...] = jnp.zeros(ref.shape, jnp.float32)
        rows_ref[...] = jnp.zeros(rows_ref.shape, jnp.float32)
        check_ref[...] = jnp.zeros(check_ref.shape, jnp.float32)
        rows_ref[8:9, :] = build(0, block1_ref)
        rows_ref[16:17, :] = build(second_node(0), block2_ref)

        def advance(index):
            @pl.when(index == outer)
            def _():
                message = carried_ref[WIDTH:]
                saved_ref[...] = lost2_ref[...]
                rows_ref[24:32, :] = message * rows_ref[33:34, :] + product(message, rest2_ref[...])
                eye = spread(ones, mask)
                lost2_ref[...] = spread(damping[0], mask)
                rest2_ref[...] = jnp.zeros((WIDTH, WIDTH), jnp.float32)
                rows_ref[33:35, :] = jnp.ones((2, WIDTH), jnp.float32)
                carried_ref[:WIDTH] = eye
                carried_ref[WIDTH:] = jnp.zeros((8, WIDTH), jnp.float32)
                far_ref[:WIDTH] = -eye
                far_ref[WIDTH:] = jnp.zeros((8, WIDTH), jnp.float32)

            excess1 = block1_ref[...] + lost1_ref[...]
            excess2 = block2_ref[...] + lost2_ref[...]
            diagonal1, diagonal2 = rows_ref[32:33, :], rows_ref[33:34, :]
            before = rows_ref[0:8, :]
            info1 = rows_ref[8:16, :] + before * diagonal1 + product(before, rest1_ref[...])
            kept = rows_ref[34:35, :]
            moved, left = eliminate(
                carried_ref[...], kept, rest2_ref[...], diagonal2, mask, product
            )
            rows_ref[34:35, :] = kept * diagonal2
            far_ref[...] += left
            carried_ref[:WIDTH] = moved[:WIDTH]
            info2 = moved[WIDTH:] + rows_ref[16:24, :]
            carried_ref[WIDTH:] = info2
            rows_ref[0:8, :] = info1
            return excess1, excess2, info1, info2

        def body(index, _):
            excess1, excess2, _, _ = advance(index)
            rows_ref[8:9, :] = build(index + 1, block1_ref)
            rows_ref[16:17, :] = build(second_node(index + 1), block2_ref)
            next1 = invert_chain(excess1, base, damping, mask)
            next2 = invert_chain(excess2, base, damping, mask)
            rest1_ref[...], rows_ref[32:33, :], lost1_ref[...] = next1
            rest2_ref[...], rows_ref[33:34, :], lost2_ref[...] = next2
            return 0

        lax.fori_loop(0, half - 1, body, 0)
        excess1, excess2, info1, info2 = advance(half - 1)
        rest, diagonal, _ = invert_middle(excess1 - far_ref[:WIDTH], base, damping, mask)
        carried_ref[:WIDTH] = carried_ref[:WIDTH].T
        carried_ref[WIDTH:] = info1 + far_ref[WIDTH:]
        _, left = eliminate(carried_ref[...], rows_ref[34:35, :], rest, diagonal, mask, product)
        excess = excess2 + saved_ref[...] - left[:WIDTH]
        info = info2 + rows_ref[24:32, :] + left[WIDTH:]

        block = cov_ref.shape[0]
        cosine = phase_ref[node, 0:1, :] * MODES
        sine = phase_ref[node, 1:2, :] * (-MODES)
        even = jnp.concatenate([cosine, -sine], axis=1)
        odd = jnp.concatenate([sine, cosine], axis=1)

        def turn_back(rows, start):
            row = iota((rows, WIDTH), 0) + start
            lane = iota((rows, WIDTH), 1) & (MODES - 1)
            value = jnp.where((row & 1) == 0, even, odd)
            return jnp.where(lane == (row >> 1), value, 0.0)

        mine = turn_back(block, shard * block)
        whole = split(turn_back(WIDTH, 0))
        (result,) = finish(excess, own_base, jnp.concatenate([mine, info], axis=0), mask)
        mean_ref[...] = dot3(split(result[block:]), split(mine), NT)[0:1]
        cov_ref[...] = dot3(split(result[:block]), whole, NT)

    def noted(inverse, row):
        def call(*args):
            *value, measure = inverse(*args)
            check_ref[row : row + 1, :] = jnp.maximum(check_ref[row : row + 1, :], measure)
            return value

        return call

    run(noted(chain_inverse, 0), noted(final_inverse, 1), noted(final_rows, 1), product3)
    chain, final = jnp.sum(check_ref[0:1, :]), jnp.sum(check_ref[1:2, :])
    flag_ref[0] = jnp.where((chain <= CHAIN_LIMIT) & (final <= FINAL_LIMIT), 1, 0)


def solve(place, stats, frequencies, decay, proc_var, block):
    square = pltpu.VMEM((WIDTH, WIDTH), jnp.float32)
    tall = pltpu.VMEM((WIDTH + 8, WIDTH), jnp.float32)
    vmem = pl.BlockSpec(memory_space=pltpu.VMEM)
    return pl.pallas_call(
        solve_kernel,
        out_shape=(
            jax.ShapeDtypeStruct((1, block), jnp.float32),
            jax.ShapeDtypeStruct((block, WIDTH), jnp.float32),
            jax.ShapeDtypeStruct((1,), jnp.int32),
        ),
        in_specs=[pl.BlockSpec(memory_space=pltpu.SMEM)] + [vmem] * 4,
        out_specs=(vmem, vmem, pl.BlockSpec(memory_space=pltpu.SMEM)),
        scratch_shapes=[
            pltpu.VMEM((stats.shape[0], 8, MODES), jnp.float32),
            *[square] * 7,
            tall,
            tall,
            pltpu.VMEM((40, WIDTH), jnp.float32),
            pltpu.VMEM((WIDTH, 8), jnp.float32),
            pltpu.VMEM((2, WIDTH), jnp.float32),
        ],
        compiler_params=pltpu.CompilerParams(vmem_limit_bytes=48 << 20),
        name="solve",
    )(place, stats, frequencies[None], decay[None], proc_var[None])


def newton_inverse(matrix):
    eye = jnp.eye(WIDTH, dtype=jnp.float32)
    start = eye / jnp.sum(jnp.abs(matrix), axis=1, keepdims=True)

    def step(_, approx):
        return approx + exact_dot(approx, eye - exact_dot(matrix, approx))

    return lax.fori_loop(0, NEWTON_STEPS, step, start)


def general(place, stats, frequencies, decay, proc_var, block):
    steps = stats.shape[0]
    time, shard = place[0], place[1]
    damping = jnp.exp(-decay)
    scale = jnp.sqrt(proc_var / damping)
    twice = jnp.concatenate([damping, damping])
    order = jnp.arange(1, MODES + 1)
    apart, together = order[:, None] - order[None, :], order[:, None] + order[None, :]
    direction = jnp.sign(apart).astype(jnp.float32)

    def node(index):
        rows = stats[index]
        even = jnp.concatenate([rows[0], rows[4, :1], rows[2, :1], rows[2, :0:-1]])
        odd = jnp.concatenate([rows[1], rows[5, :1], rows[3, :1], rows[3, :0:-1]])
        angle = index.astype(jnp.float32) * frequencies
        u_re, u_im = scale / MODES * jnp.cos(angle), -scale / MODES * jnp.sin(angle)
        t_re, t_im = even[jnp.abs(apart)], direction * odd[jnp.abs(apart)]
        h_re, h_im = even[together], odd[together]
        a_re, a_im = t_re * u_re + t_im * u_im, t_im * u_re - t_re * u_im
        b_re, b_im = h_re * u_re - h_im * u_im, h_im * u_re + h_re * u_im
        c_re, c_im = u_re[:, None], u_im[:, None]
        p_re, p_im, m_re, m_im = a_re + b_re, a_im + b_im, a_re - b_re, a_im - b_im
        upper = jnp.concatenate([c_re * p_re - c_im * p_im, -(c_re * m_im + c_im * m_re)], axis=1)
        lower = jnp.concatenate([c_re * p_im + c_im * p_re, c_re * m_re - c_im * m_im], axis=1)
        factor = MODES / (OBS_VAR * math.sqrt(MODES))
        o_re, o_im = rows[6] * factor, rows[7] * factor
        info = jnp.concatenate([o_re * u_re - o_im * u_im, o_re * u_im + o_im * u_re])
        return jnp.concatenate([upper, lower], axis=0), info

    def passed(index, state):
        lost, message = state
        precision, info = node(index)
        excess = precision + lost
        inverse = newton_inverse(jnp.diag(1.0 / twice) + excess)
        lost = twice[:, None] * exact_dot(excess, inverse)
        return 0.5 * (lost + lost.T), exact_dot(inverse, info + message)

    start = (jnp.zeros((WIDTH, WIDTH), jnp.float32), jnp.zeros((WIDTH,), jnp.float32))
    before = lax.fori_loop(0, time, passed, start)
    after = lax.fori_loop(
        0, steps - 1 - time, lambda index, state: passed(steps - 1 - index, state), start
    )
    precision, info = node(time)
    base = jnp.diag((1.0 - twice * twice) / twice)
    inverse = newton_inverse(base + precision + before[0] + after[0])
    angle = time.astype(jnp.float32) * frequencies
    cosine, sine = jnp.diag(scale * jnp.cos(angle)), jnp.diag(scale * jnp.sin(angle))
    back = jnp.stack(
        [jnp.concatenate([cosine, -sine], axis=1), jnp.concatenate([sine, cosine], axis=1)], axis=1
    ).reshape(WIDTH, WIDTH)
    mine = exact_dot(lax.dynamic_slice_in_dim(back, shard * block, block, 0), inverse)
    mean = exact_dot(mine, info + before[1] + after[1])
    return mean[None], exact_dot(mine, back, NT)


def statistics(site_row, obs_row, count, copies):
    transform, twiddles = tables()
    vmem = pl.BlockSpec(memory_space=pltpu.VMEM)
    return pl.pallas_call(
        statistics_kernel,
        out_shape=jax.ShapeDtypeStruct((copies, 8, MODES), jnp.float32),
        in_specs=[pl.BlockSpec(memory_space=pltpu.SMEM)] + [vmem] * 4,
        out_specs=vmem,
        name="statistics",
    )(count, site_row, obs_row, jnp.asarray(transform), jnp.asarray(twiddles))


def local(observations, site_ids, counts, frequencies, decay, proc_var):
    steps = lax.axis_size("tm")
    block = WIDTH // lax.axis_size("rows")
    copies = statistics(site_ids, observations, counts, steps)
    everyone = lax.all_to_all(copies, "tm", split_axis=0, concat_axis=0, tiled=True)
    place = jnp.stack([lax.axis_index("tm"), lax.axis_index("rows")]).astype(jnp.int32)
    mean, cov, flag = solve(place, everyone, frequencies, decay, proc_var, block)
    mean, cov = lax.cond(
        flag[0] == 1,
        lambda place, everyone, mean, cov: (mean, cov),
        lambda place, everyone, mean, cov: general(
            place, everyone, frequencies, decay, proc_var, block
        ),
        place,
        everyone,
        mean,
        cov,
    )
    return mean, cov[None]


def solution(mesh):
    return jax.shard_map(
        local,
        mesh=mesh,
        in_specs=(P("tm", None), P("tm", None), P("tm"), P(), P(), P()),
        out_specs=(P("tm", "rows"), P("tm", "rows", None)),
        check_vma=False,
    )
```
